256 devices in a mesh: gx: 16 (over z_lo, y), gy: 8 (over x, core), ta: 2 (over z_hi).
Axes of the slice: x: 4, y: 4, z: 8 (z_hi: 2, z_lo: 4; z = z_hi * 4 + z_lo), core: 2. Of those that a mesh axis runs over, the one named last changes fastest.
Arguments:
- eigvecs: bfloat16 [2, 16, 64, 64, 3, 256], P('ta', 'gx', 'gy'), may hold values from -6 to 6
- links: bfloat16 [2, 16, 64, 3, 3, 3, 128], P('ta', 'gx', 'gy'), may hold values from -3.5 to 3.5
- momenta: int32 [8, 3], replicated, may hold values from -2 to 2
- directions: int32 [8], replicated, may hold values from 0 to 2, as said below
- pairs: int32 [512, 2], P(('gx', 'gy', 'ta')), may hold values from 0 to 1
- perambulators: float32 [512, 128, 256], P(('gx', 'gy', 'ta')), may hold values from -0.5 to 0.5
Outputs:
- fields: float32 [2, 8, 128, 256], P('ta')
- correlators: float32 [512, 64], P(('gx', 'gy', 'ta'))
The draws below stay inside these ranges and needn't reach their ends.
Inputs may be any that keep to these rules, and one draw needn't show every extreme that they name: Each of the three directions is named by at least one operator.
All inputs are finite; a program needn't handle non-finite values.
Results may differ from the reference program's by a relative error of at most 0.0063.
Values may be sent and summed in bfloat16 or wider, within the bound.
A program may use at most 64 MiB of HBM per device.

```python
import math
import jax
import jax.numpy as jnp
from jax import lax

NEV = 128
OPS = 8
NZ = 64
NX = 16
NY = 64
T_SIZE = 2
NPAIRS = 512


def draw_directions(key, part):
    first_three = jax.random.permutation(jax.random.fold_in(key, 11), 3).astype(jnp.int32)
    remaining = jax.random.randint(jax.random.fold_in(key, 12), (OPS - 3,), 0, 3, dtype=jnp.int32)
    return jnp.concatenate([first_three, remaining]).astype(jnp.int32)


def with_ends(result, own_key, least, top_value):
    extent = result.shape
    spot = [jax.random.randint(jax.random.fold_in(own_key, axis), (), 0, extent[axis]) for axis in range(len(extent))]
    result = result.at[tuple(spot)].set(least)
    longest = extent.index(max(extent))
    spot[longest] = (spot[longest] + 1) % extent[longest]
    return result.at[tuple(spot)].set(top_value)


def levels(key, shape, cuts, low, top_value):
    def one(axis_at, blocks):
        steps = jax.random.uniform(jax.random.fold_in(jax.random.fold_in(key, 6), axis_at), (blocks,), jnp.float32, low / len(cuts), top_value / len(cuts))
        return jnp.repeat(jnp.exp(steps), shape[axis_at] // blocks).reshape((-1,) + (1,) * (len(shape) - axis_at - 1))

    factor_of = one(*cuts[0])
    for cut in cuts[1:]:
        factor_of = factor_of * one(*cut)
    return factor_of


def bell_draw(own_key, shape, spread, bound, shards=(), kind=jnp.bfloat16):
    loudness = levels(own_key, shape, shards, -0.22, 0.18) if shards else 1.0
    entries = jax.random.normal(own_key, shape, jnp.float32) * spread * loudness
    return jnp.minimum(jnp.maximum(entries, -bound), bound).astype(kind)


def setup_inputs(seed: int = 0) -> dict:
    splits = jax.random.split(jax.random.key(seed), 7)
    return {
        "eigvecs": bell_draw(splits[0], (T_SIZE, NX, NY, NZ, 3, 2 * NEV), 1.0, 6.0, ((0, 2), (1, 16), (2, 8))),
        "links": bell_draw(splits[1], (T_SIZE, NX, NY, 3, 3, 3, 2 * NZ), 3 ** -0.5, 3.5, ((0, 2), (1, 16), (2, 8))),
        "momenta": with_ends(jax.random.randint(splits[2], (OPS, 3), -2, 3), jax.random.fold_in(splits[2], 1), -2, 2).astype(jnp.int32),
        "directions": draw_directions(jax.random.fold_in(splits[6], 71), 0),
        "pairs": with_ends(jax.random.randint(splits[4], (NPAIRS, 2), 0, T_SIZE), jax.random.fold_in(splits[4], 1), 0, T_SIZE - 1).astype(jnp.int32),
        "perambulators": bell_draw(splits[5], (NPAIRS, NEV, 2 * NEV), NEV ** -0.5, 0.5, ((0, 256),), jnp.float32),
    }


def color_apply(real_links, imag_links, vectors, dagger):
    pattern = '...ba,...bpk->...apk' if dagger else '...ab,...bpk->...apk'
    vec_wide = vectors.astype(jnp.float32)
    real_term = jnp.einsum(pattern, real_links.astype(jnp.float32), vec_wide)
    imag_term = jnp.einsum(pattern, imag_links.astype(jnp.float32), vec_wide)
    if dagger:
        imag_term = -imag_term
    real_out = real_term[..., 0, :] - imag_term[..., 1, :]
    imag_out = real_term[..., 1, :] + imag_term[..., 0, :]
    return jnp.stack([real_out, imag_out], axis=-2)

def phase_parts(momentum, coord_x, coord_y, coord_z, span_x, span_y, span_z):
    fraction = (jnp.mod(momentum[0] * coord_x, span_x).astype(jnp.float32) / span_x)[:, None, None]
    fraction = fraction + (jnp.mod(momentum[1] * coord_y, span_y).astype(jnp.float32) / span_y)[None, :, None]
    fraction = fraction + (jnp.mod(momentum[2] * coord_z, span_z).astype(jnp.float32) / span_z)[None, None, :]
    phase_angle = 2.0 * math.pi * fraction
    return (jnp.cos(phase_angle)[..., None, None], jnp.sin(phase_angle)[..., None, None])

def complex_product(left_side, right_side):
    half_width = left_side.shape[-2]
    highest = lax.Precision.HIGHEST
    left_real, left_imag = (left_side[..., :half_width], left_side[..., half_width:])
    right_real, right_imag = (right_side[..., :half_width], right_side[..., half_width:])
    real_out = jnp.matmul(left_real, right_real, precision=highest) - jnp.matmul(left_imag, right_imag, precision=highest)
    imag_out = jnp.matmul(left_real, right_imag, precision=highest) + jnp.matmul(left_imag, right_real, precision=highest)
    return jnp.concatenate([real_out, imag_out], axis=-1)

def reference(eigvecs, links, momenta, directions, pairs, perambulators):
    mode_count = NEV
    scale_norm = 1.0 / math.sqrt(3 * NX * NY * NZ)

    def one_slice(inputs):
        eig_slice, link_slice = inputs
        vectors = eig_slice.reshape(NX, NY, NZ, 3, 2, mode_count)
        split = link_slice.reshape(NX, NY, 3, 3, 3, 2, NZ)
        moved = jnp.transpose(split, (2, 5, 0, 1, 6, 3, 4))
        displaced_list = []
        for axis_dir in range(3):
            forward = color_apply(moved[axis_dir, 0], moved[axis_dir, 1], jnp.roll(vectors, -1, axis=axis_dir), False)
            backward = color_apply(moved[axis_dir, 0], moved[axis_dir, 1], vectors, True).astype(jnp.bfloat16)
            shifted = jnp.roll(backward, 1, axis=axis_dir).astype(jnp.float32)
            displaced_list.append((forward - shifted).astype(jnp.bfloat16))
        stacked = jnp.stack(displaced_list)
        coord_x = jnp.arange(NX, dtype=jnp.int32)
        coord_y = jnp.arange(NY, dtype=jnp.int32)
        coord_z = jnp.arange(NZ, dtype=jnp.int32)
        vec_real = vectors[..., 0, :].astype(jnp.float32)
        vec_imag = vectors[..., 1, :].astype(jnp.float32)
        results = []
        for op_index in range(OPS):
            cosine, sine_part = phase_parts(momenta[op_index], coord_x, coord_y, coord_z, NX, NY, NZ)
            real_part = vec_real * cosine - vec_imag * sine_part
            imag_part = -(vec_imag * cosine + vec_real * sine_part)
            weighted = jnp.stack([real_part, imag_part], axis=-2).astype(jnp.bfloat16)
            chosen = lax.dynamic_index_in_dim(stacked, directions[op_index], 0, keepdims=False)
            blocks = jnp.einsum('xyzcpk,xyzcqm->pkqm', weighted.astype(jnp.float32), chosen.astype(jnp.float32))
            field_real = blocks[0, :, 0, :] - blocks[1, :, 1, :]
            field_imag = blocks[0, :, 1, :] + blocks[1, :, 0, :]
            results.append(jnp.concatenate([field_real, field_imag], axis=-1))
        return jnp.stack(results)
    fields = lax.map(one_slice, (eigvecs, links)) * scale_norm
    sink_field = fields[pairs[:, 0]]
    source_field = fields[pairs[:, 1]]
    propagator = perambulators[:, None]
    left_product = complex_product(sink_field, propagator)
    right_product = complex_product(propagator, source_field)
    correlator = jnp.einsum('paij,pbij->pab', left_product, right_product, precision=lax.Precision.HIGHEST)
    correlator = (correlator / (mode_count * mode_count)).reshape(pairs.shape[0], OPS * OPS)
    return (fields, correlator)
```

```python
import math

import jax
import jax.numpy as jnp
from jax import lax
from jax.sharding import PartitionSpec as P


def from_behind(value, axis, steps):
    count = lax.axis_size(axis)
    pairs = [(source, (source + steps) % count) for source in range(count)]
    return lax.ppermute(value, axis, pairs)


def partner_pairs(axis, bit):
    return [(index, index ^ (1 << bit)) for index in range(lax.axis_size(axis))]


def halving_sum(value, spread):
    for axis, bit in spread:
        upper = (lax.axis_index(axis) >> bit) & 1
        half = value.shape[0] // 2
        keep = lax.dynamic_slice_in_dim(value, upper * half, half, 0)
        send = lax.dynamic_slice_in_dim(value, (1 - upper) * half, half, 0)
        value = keep + lax.ppermute(send, axis, partner_pairs(axis, bit))
    return value


def doubling_gather(value, spread):
    for axis, bit in reversed(spread):
        upper = (lax.axis_index(axis) >> bit) & 1
        got = lax.ppermute(value, axis, partner_pairs(axis, bit))
        value = jnp.where(
            upper == 0, jnp.concatenate([value, got], 0), jnp.concatenate([got, value], 0)
        )
    return value


def link_parts(raw_links):
    slice_count, wide_x, wide_y = (raw_links.shape[0], raw_links.shape[1], raw_links.shape[2])
    z_count = raw_links.shape[-1] // 2
    split = raw_links.reshape(slice_count, wide_x, wide_y, 3, 3, 3, 2, z_count)
    moved = jnp.transpose(split, (3, 6, 0, 1, 2, 7, 4, 5))
    return (moved[:, 0], moved[:, 1])


def color_apply(real_links, imag_links, vectors, dagger):
    pattern = "...ba,...bpk->...apk" if dagger else "...ab,...bpk->...apk"
    real_term = jnp.einsum(pattern, real_links, vectors, preferred_element_type=jnp.float32)
    imag_term = jnp.einsum(pattern, imag_links, vectors, preferred_element_type=jnp.float32)
    if dagger:
        imag_term = -imag_term
    real_out = real_term[..., 0, :] - imag_term[..., 1, :]
    imag_out = real_term[..., 1, :] + imag_term[..., 0, :]
    return jnp.stack([real_out, imag_out], axis=-2)


def phase_parts(momentum, coord_x, coord_y, coord_z, span_x, span_y, span_z):
    fraction = (jnp.mod(momentum[0] * coord_x, span_x).astype(jnp.float32) / span_x)[:, None, None]
    fraction = (
        fraction
        + (jnp.mod(momentum[1] * coord_y, span_y).astype(jnp.float32) / span_y)[None, :, None]
    )
    fraction = (
        fraction
        + (jnp.mod(momentum[2] * coord_z, span_z).astype(jnp.float32) / span_z)[None, None, :]
    )
    phase_angle = 2.0 * math.pi * fraction
    return (jnp.cos(phase_angle)[..., None, None], jnp.sin(phase_angle)[..., None, None])


def complex_product(left_side, right_side):
    half_width = left_side.shape[-2]
    highest = lax.Precision.HIGHEST
    left_real, left_imag = (left_side[..., :half_width], left_side[..., half_width:])
    right_real, right_imag = (right_side[..., :half_width], right_side[..., half_width:])
    real_out = jnp.matmul(left_real, right_real, precision=highest) - jnp.matmul(
        left_imag, right_imag, precision=highest
    )
    imag_out = jnp.matmul(left_real, right_imag, precision=highest) + jnp.matmul(
        left_imag, right_real, precision=highest
    )
    return jnp.concatenate([real_out, imag_out], axis=-1)


def local(eigvecs, links, momenta, directions, pairs, perambulators):
    slices, cells_x, cells_y, cells_z = (
        eigvecs.shape[0],
        eigvecs.shape[1],
        eigvecs.shape[2],
        eigvecs.shape[3],
    )
    mode_count = eigvecs.shape[-1] // 2
    op_count = momenta.shape[0]
    span_x = cells_x * lax.axis_size("gx")
    span_y = cells_y * lax.axis_size("gy")
    scale_norm = 1.0 / math.sqrt(3 * span_x * span_y * cells_z)
    vectors = eigvecs.reshape(slices, cells_x, cells_y, cells_z, 3, 2, mode_count)
    real_links, imag_links = link_parts(links)
    ahead_x = from_behind(eigvecs, "gx", -1)
    next_x = jnp.concatenate(
        [vectors[:, 1:], ahead_x.reshape(slices, 1, cells_y, cells_z, 3, 2, mode_count)], axis=1
    )
    back_x = color_apply(real_links[0], imag_links[0], vectors, True).astype(jnp.bfloat16)
    behind_x = from_behind(back_x, "gx", 1)
    prev_x = jnp.concatenate([behind_x, back_x[:, :-1]], axis=1)
    ahead_y = from_behind(eigvecs[:, :, :1], "gy", -1)
    next_y = jnp.concatenate(
        [vectors[:, :, 1:], ahead_y.reshape(slices, cells_x, 1, cells_z, 3, 2, mode_count)], axis=2
    )
    back_y = color_apply(real_links[1], imag_links[1], vectors, True).astype(jnp.bfloat16)
    behind_y = from_behind(back_y[:, :, -1:], "gy", 1)
    prev_y = jnp.concatenate([behind_y, back_y[:, :, :-1]], axis=2)
    forward_x = color_apply(real_links[0], imag_links[0], next_x, False)
    displaced_x = (forward_x - prev_x).astype(jnp.bfloat16)
    forward_y = color_apply(real_links[1], imag_links[1], next_y, False)
    displaced_y = (forward_y - prev_y).astype(jnp.bfloat16)
    forward_z = color_apply(real_links[2], imag_links[2], jnp.roll(vectors, -1, axis=3), False)
    back_z = color_apply(real_links[2], imag_links[2], vectors, True).astype(jnp.bfloat16)
    displaced_z = (forward_z - jnp.roll(back_z, 1, axis=3)).astype(jnp.bfloat16)
    row_count = cells_x * cells_y * cells_z * 3
    stacked = jnp.stack([displaced_x, displaced_y, displaced_z]).reshape(
        3, slices, row_count, 2 * mode_count
    )
    coord_x = lax.axis_index("gx") * cells_x + jnp.arange(cells_x, dtype=jnp.int32)
    coord_y = lax.axis_index("gy") * cells_y + jnp.arange(cells_y, dtype=jnp.int32)
    coord_z = jnp.arange(cells_z, dtype=jnp.int32)
    vec_real = vectors[..., 0, :]
    vec_imag = vectors[..., 1, :]
    results = []
    for op_index in range(op_count):
        cosine, sine_part = phase_parts(
            momenta[op_index], coord_x, coord_y, coord_z, span_x, span_y, cells_z
        )
        real_part = vec_real * cosine - vec_imag * sine_part
        imag_part = -(vec_imag * cosine + vec_real * sine_part)
        weighted = jnp.stack([real_part, imag_part], axis=-2).astype(jnp.bfloat16)
        weighted = weighted.reshape(slices, row_count, 2 * mode_count)
        chosen = lax.dynamic_index_in_dim(stacked, directions[op_index], 0, keepdims=False)
        blocks = jnp.einsum("trk,trm->tkm", weighted, chosen, preferred_element_type=jnp.float32)
        field_real = blocks[:, :mode_count, :mode_count] - blocks[:, mode_count:, mode_count:]
        field_imag = blocks[:, :mode_count, mode_count:] + blocks[:, mode_count:, :mode_count]
        results.append(jnp.concatenate([field_real, field_imag], axis=-1))
    partial_sum = jnp.stack(results, axis=1)
    flat_sum = partial_sum.reshape(-1, partial_sum.shape[-1])
    spread = [(axis, bit) for axis in ("gy", "gx") for bit in range(lax.axis_size(axis).bit_length() - 1)]
    reduced = halving_sum(flat_sum, spread)
    own_fields = (doubling_gather(reduced, spread) * scale_norm).reshape(partial_sum.shape)
    other_field = lax.ppermute(own_fields, "ta", [(0, 1), (1, 0)])
    whole_field = jnp.where(
        lax.axis_index("ta") == 0,
        jnp.concatenate([own_fields, other_field], axis=0),
        jnp.concatenate([other_field, own_fields], axis=0),
    )
    highest = lax.Precision.HIGHEST
    time_grid = jnp.arange(whole_field.shape[0], dtype=jnp.int32)
    pick_sink = (pairs[:, 0:1] == time_grid[None, :]).astype(jnp.float32)
    pick_source = (pairs[:, 1:2] == time_grid[None, :]).astype(jnp.float32)
    sink_field = jnp.einsum("pt,toij->poij", pick_sink, whole_field, precision=highest)
    source_field = jnp.einsum("pt,toij->poij", pick_source, whole_field, precision=highest)
    propagator = perambulators[:, None]
    left_product = complex_product(sink_field, propagator)
    right_product = complex_product(propagator, source_field)
    correlator = jnp.einsum("paij,pbij->pab", left_product, right_product, precision=highest)
    correlator = (correlator / (mode_count * mode_count)).reshape(
        pairs.shape[0], op_count * op_count
    )
    return (own_fields, correlator)


def solution(mesh):
    in_specs = (
        P("ta", "gx", "gy", None, None, None),
        P("ta", "gx", "gy", None, None, None, None),
        P(),
        P(),
        P(("gx", "gy", "ta"), None),
        P(("gx", "gy", "ta"), None, None),
    )
    out_specs = (P("ta", None, None, None), P(("gx", "gy", "ta"), None))
    return jax.shard_map(local, mesh=mesh, in_specs=in_specs, out_specs=out_specs, check_vma=False)
```

```python
import math

import jax
import jax.numpy as jnp
from jax import lax
from jax.sharding import PartitionSpec as P


def from_behind(value, axis, steps):
    count = lax.axis_size(axis)
    pairs = [(source, (source + steps) % count) for source in range(count)]
    return lax.ppermute(value, axis, pairs)


def partner_pairs(axis, mask):
    return [(index, index ^ mask) for index in range(lax.axis_size(axis))]


def radix_digits(axis):
    bits = lax.axis_size(axis).bit_length() - 1
    widths = [1] * (bits % 2) + [2] * (bits // 2)
    lows = [sum(widths[:n]) for n in range(len(widths))]
    return [(axis, low, width) for low, width in zip(lows, widths)]


def digit_sum(value, digits):
    for axis, low, width in digits:
        count = 1 << width
        digit = (lax.axis_index(axis) >> low) & (count - 1)
        part = value.shape[0] // count
        total = lax.dynamic_slice_in_dim(value, digit * part, part, 0)
        for shift in range(1, count):
            send = lax.dynamic_slice_in_dim(value, (digit ^ shift) * part, part, 0)
            total = total + lax.ppermute(send, axis, partner_pairs(axis, shift << low))
        value = total
    return value


def digit_gather(value, digits):
    for axis, low, width in reversed(digits):
        count = 1 << width
        digit = (lax.axis_index(axis) >> low) & (count - 1)
        got = [value] + [
            lax.ppermute(value, axis, partner_pairs(axis, shift << low)) for shift in range(1, count)
        ]
        pieces = []
        for place in range(count):
            piece = got[0]
            for shift in range(1, count):
                piece = jnp.where((place ^ digit) == shift, got[shift], piece)
            pieces.append(piece)
        value = jnp.concatenate(pieces, 1)
    return value

def link_parts(raw_links):
    slice_count, wide_x, wide_y = (raw_links.shape[0], raw_links.shape[1], raw_links.shape[2])
    z_count = raw_links.shape[-1] // 2
    split = raw_links.reshape(slice_count, wide_x, wide_y, 3, 3, 3, 2, z_count)
    moved = jnp.transpose(split, (3, 6, 0, 1, 2, 7, 4, 5))
    return (moved[:, 0], moved[:, 1])


def color_apply(real_links, imag_links, vectors, dagger):
    pattern = "...ba,...bpk->...apk" if dagger else "...ab,...bpk->...apk"
    real_term = jnp.einsum(pattern, real_links, vectors, preferred_element_type=jnp.float32)
    imag_term = jnp.einsum(pattern, imag_links, vectors, preferred_element_type=jnp.float32)
    if dagger:
        imag_term = -imag_term
    real_out = real_term[..., 0, :] - imag_term[..., 1, :]
    imag_out = real_term[..., 1, :] + imag_term[..., 0, :]
    return jnp.stack([real_out, imag_out], axis=-2)


def phase_parts(momentum, coord_x, coord_y, coord_z, span_x, span_y, span_z):
    fraction = (jnp.mod(momentum[0] * coord_x, span_x).astype(jnp.float32) / span_x)[:, None, None]
    fraction = (
        fraction
        + (jnp.mod(momentum[1] * coord_y, span_y).astype(jnp.float32) / span_y)[None, :, None]
    )
    fraction = (
        fraction
        + (jnp.mod(momentum[2] * coord_z, span_z).astype(jnp.float32) / span_z)[None, None, :]
    )
    phase_angle = 2.0 * math.pi * fraction
    return (jnp.cos(phase_angle)[..., None, None], jnp.sin(phase_angle)[..., None, None])


def complex_product(left_side, right_side):
    half_width = left_side.shape[-2]
    highest = lax.Precision.HIGHEST
    left_real, left_imag = (left_side[..., :half_width], left_side[..., half_width:])
    right_real, right_imag = (right_side[..., :half_width], right_side[..., half_width:])
    real_out = jnp.matmul(left_real, right_real, precision=highest) - jnp.matmul(
        left_imag, right_imag, precision=highest
    )
    imag_out = jnp.matmul(left_real, right_imag, precision=highest) + jnp.matmul(
        left_imag, right_real, precision=highest
    )
    return jnp.concatenate([real_out, imag_out], axis=-1)


def local(eigvecs, links, momenta, directions, pairs, perambulators):
    slices, cells_x, cells_y, cells_z = (
        eigvecs.shape[0],
        eigvecs.shape[1],
        eigvecs.shape[2],
        eigvecs.shape[3],
    )
    mode_count = eigvecs.shape[-1] // 2
    op_count = momenta.shape[0]
    span_x = cells_x * lax.axis_size("gx")
    span_y = cells_y * lax.axis_size("gy")
    scale_norm = 1.0 / math.sqrt(3 * span_x * span_y * cells_z)
    vectors = eigvecs.reshape(slices, cells_x, cells_y, cells_z, 3, 2, mode_count)
    real_links, imag_links = link_parts(links)
    ahead_x = from_behind(eigvecs, "gx", -1)
    next_x = jnp.concatenate(
        [vectors[:, 1:], ahead_x.reshape(slices, 1, cells_y, cells_z, 3, 2, mode_count)], axis=1
    )
    back_x = color_apply(real_links[0], imag_links[0], vectors, True).astype(jnp.bfloat16)
    behind_x = from_behind(back_x, "gx", 1)
    prev_x = jnp.concatenate([behind_x, back_x[:, :-1]], axis=1)
    ahead_y = from_behind(eigvecs[:, :, :1], "gy", -1)
    next_y = jnp.concatenate(
        [vectors[:, :, 1:], ahead_y.reshape(slices, cells_x, 1, cells_z, 3, 2, mode_count)], axis=2
    )
    back_y = color_apply(real_links[1], imag_links[1], vectors, True).astype(jnp.bfloat16)
    behind_y = from_behind(back_y[:, :, -1:], "gy", 1)
    prev_y = jnp.concatenate([behind_y, back_y[:, :, :-1]], axis=2)
    forward_x = color_apply(real_links[0], imag_links[0], next_x, False)
    displaced_x = (forward_x - prev_x).astype(jnp.bfloat16)
    forward_y = color_apply(real_links[1], imag_links[1], next_y, False)
    displaced_y = (forward_y - prev_y).astype(jnp.bfloat16)
    forward_z = color_apply(real_links[2], imag_links[2], jnp.roll(vectors, -1, axis=3), False)
    back_z = color_apply(real_links[2], imag_links[2], vectors, True).astype(jnp.bfloat16)
    displaced_z = (forward_z - jnp.roll(back_z, 1, axis=3)).astype(jnp.bfloat16)
    row_count = cells_x * cells_y * cells_z * 3
    stacked = jnp.stack([displaced_x, displaced_y, displaced_z]).reshape(
        3, slices, row_count, 2 * mode_count
    )
    coord_x = lax.axis_index("gx") * cells_x + jnp.arange(cells_x, dtype=jnp.int32)
    coord_y = lax.axis_index("gy") * cells_y + jnp.arange(cells_y, dtype=jnp.int32)
    coord_z = jnp.arange(cells_z, dtype=jnp.int32)
    vec_real = vectors[..., 0, :]
    vec_imag = vectors[..., 1, :]
    results = []
    for op_index in range(op_count):
        cosine, sine_part = phase_parts(
            momenta[op_index], coord_x, coord_y, coord_z, span_x, span_y, cells_z
        )
        real_part = vec_real * cosine - vec_imag * sine_part
        imag_part = -(vec_imag * cosine + vec_real * sine_part)
        weighted = jnp.stack([real_part, imag_part], axis=-2).astype(jnp.bfloat16)
        weighted = weighted.reshape(slices, row_count, 2 * mode_count)
        chosen = lax.dynamic_index_in_dim(stacked, directions[op_index], 0, keepdims=False)
        blocks = jnp.einsum("trk,trm->tkm", weighted, chosen, preferred_element_type=jnp.float32)
        field_real = blocks[:, :mode_count, :mode_count] - blocks[:, mode_count:, mode_count:]
        field_imag = blocks[:, :mode_count, mode_count:] + blocks[:, mode_count:, :mode_count]
        results.append(jnp.concatenate([field_real, field_imag], axis=-1))
    partial_sum = jnp.stack(results, axis=1)
    flat_sum = partial_sum.reshape(-1, partial_sum.shape[-1])
    digits = radix_digits("gy") + radix_digits("gx")
    reduced = digit_sum(flat_sum, digits)
    other_part = lax.ppermute(reduced, "ta", [(0, 1), (1, 0)])
    both_parts = jnp.where(
        lax.axis_index("ta") == 0,
        jnp.stack([reduced, other_part]),
        jnp.stack([other_part, reduced]),
    )
    whole_field = (digit_gather(both_parts, digits) * scale_norm).reshape(
        (2,) + partial_sum.shape[1:]
    )
    own_fields = lax.dynamic_index_in_dim(whole_field, lax.axis_index("ta"), 0, keepdims=True)
    highest = lax.Precision.HIGHEST
    time_grid = jnp.arange(whole_field.shape[0], dtype=jnp.int32)
    pick_sink = (pairs[:, 0:1] == time_grid[None, :]).astype(jnp.float32)
    pick_source = (pairs[:, 1:2] == time_grid[None, :]).astype(jnp.float32)
    sink_field = jnp.einsum("pt,toij->poij", pick_sink, whole_field, precision=highest)
    source_field = jnp.einsum("pt,toij->poij", pick_source, whole_field, precision=highest)
    propagator = perambulators[:, None]
    left_product = complex_product(sink_field, propagator)
    right_product = complex_product(propagator, source_field)
    correlator = jnp.einsum("paij,pbij->pab", left_product, right_product, precision=highest)
    correlator = (correlator / (mode_count * mode_count)).reshape(
        pairs.shape[0], op_count * op_count
    )
    return (own_fields, correlator)


def solution(mesh):
    in_specs = (
        P("ta", "gx", "gy", None, None, None),
        P("ta", "gx", "gy", None, None, None, None),
        P(),
        P(),
        P(("gx", "gy", "ta"), None),
        P(("gx", "gy", "ta"), None, None),
    )
    out_specs = (P("ta", None, None, None), P(("gx", "gy", "ta"), None))
    return jax.shard_map(local, mesh=mesh, in_specs=in_specs, out_specs=out_specs, check_vma=False)
```

```python
import math

import jax
import jax.numpy as jnp
from jax import lax
from jax.sharding import PartitionSpec as P


def from_behind(value, axis, steps):
    count = lax.axis_size(axis)
    pairs = [(source, (source + steps) % count) for source in range(count)]
    return lax.ppermute(value, axis, pairs)


def partner_pairs(axis, mask):
    return [(index, index ^ mask) for index in range(lax.axis_size(axis))]


def radix_digits(axis):
    bits = lax.axis_size(axis).bit_length() - 1
    widths = [1] * (bits % 2) + [2] * (bits // 2)
    lows = [sum(widths[:n]) for n in range(len(widths))]
    return [(axis, low, width) for low, width in zip(lows, widths)]


def digit_sum(value, digits):
    for axis, low, width in digits:
        count = 1 << width
        digit = (lax.axis_index(axis) >> low) & (count - 1)
        part = value.shape[0] // count
        total = lax.dynamic_slice_in_dim(value, digit * part, part, 0)
        for shift in range(1, count):
            send = lax.dynamic_slice_in_dim(value, (digit ^ shift) * part, part, 0)
            total = total + lax.ppermute(send, axis, partner_pairs(axis, shift << low))
        value = total
    return value


def digit_gather(value, digits):
    for axis, low, width in reversed(digits):
        count = 1 << width
        digit = (lax.axis_index(axis) >> low) & (count - 1)
        got = [value] + [
            lax.ppermute(value, axis, partner_pairs(axis, shift << low)) for shift in range(1, count)
        ]
        pieces = []
        for place in range(count):
            piece = got[0]
            for shift in range(1, count):
                piece = jnp.where((place ^ digit) == shift, got[shift], piece)
            pieces.append(piece)
        value = jnp.concatenate(pieces, 1)
    return value

def link_parts(raw_links):
    slice_count, wide_x, wide_y = (raw_links.shape[0], raw_links.shape[1], raw_links.shape[2])
    z_count = raw_links.shape[-1] // 2
    split = raw_links.reshape(slice_count, wide_x, wide_y, 3, 3, 3, 2, z_count)
    moved = jnp.transpose(split, (3, 6, 0, 1, 2, 7, 4, 5))
    return (moved[:, 0], moved[:, 1])


def color_apply(real_links, imag_links, vectors, dagger):
    pattern = "...ba,...bpk->...apk" if dagger else "...ab,...bpk->...apk"
    real_term = jnp.einsum(pattern, real_links, vectors, preferred_element_type=jnp.float32)
    imag_term = jnp.einsum(pattern, imag_links, vectors, preferred_element_type=jnp.float32)
    if dagger:
        imag_term = -imag_term
    real_out = real_term[..., 0, :] - imag_term[..., 1, :]
    imag_out = real_term[..., 1, :] + imag_term[..., 0, :]
    return jnp.stack([real_out, imag_out], axis=-2)


def phase_parts(momentum, coord_x, coord_y, coord_z, span_x, span_y, span_z):
    fraction = (jnp.mod(momentum[0] * coord_x, span_x).astype(jnp.float32) / span_x)[:, None, None]
    fraction = (
        fraction
        + (jnp.mod(momentum[1] * coord_y, span_y).astype(jnp.float32) / span_y)[None, :, None]
    )
    fraction = (
        fraction
        + (jnp.mod(momentum[2] * coord_z, span_z).astype(jnp.float32) / span_z)[None, None, :]
    )
    phase_angle = 2.0 * math.pi * fraction
    return (jnp.cos(phase_angle)[..., None, None], jnp.sin(phase_angle)[..., None, None])


def complex_product(left_side, right_side):
    half_width = left_side.shape[-2]
    highest = lax.Precision.HIGHEST
    left_real, left_imag = (left_side[..., :half_width], left_side[..., half_width:])
    right_real, right_imag = (right_side[..., :half_width], right_side[..., half_width:])
    real_out = jnp.matmul(left_real, right_real, precision=highest) - jnp.matmul(
        left_imag, right_imag, precision=highest
    )
    imag_out = jnp.matmul(left_real, right_imag, precision=highest) + jnp.matmul(
        left_imag, right_real, precision=highest
    )
    return jnp.concatenate([real_out, imag_out], axis=-1)


def local(eigvecs, links, momenta, directions, pairs, perambulators):
    slices, cells_x, cells_y, cells_z = (
        eigvecs.shape[0],
        eigvecs.shape[1],
        eigvecs.shape[2],
        eigvecs.shape[3],
    )
    mode_count = eigvecs.shape[-1] // 2
    op_count = momenta.shape[0]
    span_x = cells_x * lax.axis_size("gx")
    span_y = cells_y * lax.axis_size("gy")
    scale_norm = 1.0 / math.sqrt(3 * span_x * span_y * cells_z)
    vectors = eigvecs.reshape(slices, cells_x, cells_y, cells_z, 3, 2, mode_count)
    real_links, imag_links = link_parts(links)
    ahead_x = from_behind(eigvecs, "gx", -1)
    next_x = jnp.concatenate(
        [vectors[:, 1:], ahead_x.reshape(slices, 1, cells_y, cells_z, 3, 2, mode_count)], axis=1
    )
    back_x = color_apply(real_links[0], imag_links[0], vectors, True).astype(jnp.bfloat16)
    behind_x = from_behind(back_x, "gx", 1)
    prev_x = jnp.concatenate([behind_x, back_x[:, :-1]], axis=1)
    ahead_y = from_behind(eigvecs[:, :, :1], "gy", -1)
    next_y = jnp.concatenate(
        [vectors[:, :, 1:], ahead_y.reshape(slices, cells_x, 1, cells_z, 3, 2, mode_count)], axis=2
    )
    back_y = color_apply(real_links[1], imag_links[1], vectors, True).astype(jnp.bfloat16)
    behind_y = from_behind(back_y[:, :, -1:], "gy", 1)
    prev_y = jnp.concatenate([behind_y, back_y[:, :, :-1]], axis=2)
    forward_x = color_apply(real_links[0], imag_links[0], next_x, False)
    displaced_x = (forward_x - prev_x).astype(jnp.bfloat16)
    forward_y = color_apply(real_links[1], imag_links[1], next_y, False)
    displaced_y = (forward_y - prev_y).astype(jnp.bfloat16)
    forward_z = color_apply(real_links[2], imag_links[2], jnp.roll(vectors, -1, axis=3), False)
    back_z = color_apply(real_links[2], imag_links[2], vectors, True).astype(jnp.bfloat16)
    displaced_z = (forward_z - jnp.roll(back_z, 1, axis=3)).astype(jnp.bfloat16)
    row_count = cells_x * cells_y * cells_z * 3
    stacked = jnp.stack([displaced_x, displaced_y, displaced_z]).reshape(
        3, slices, row_count, 2 * mode_count
    )
    coord_x = lax.axis_index("gx") * cells_x + jnp.arange(cells_x, dtype=jnp.int32)
    coord_y = lax.axis_index("gy") * cells_y + jnp.arange(cells_y, dtype=jnp.int32)
    coord_z = jnp.arange(cells_z, dtype=jnp.int32)
    cosine, sine_part = jax.vmap(
        lambda momentum: phase_parts(momentum, coord_x, coord_y, coord_z, span_x, span_y, cells_z)
    )(momenta)
    vec_real = vectors[0, ..., 0, :][None]
    vec_imag = vectors[0, ..., 1, :][None]
    real_part = vec_real * cosine - vec_imag * sine_part
    imag_part = -(vec_imag * cosine + vec_real * sine_part)
    weighted = jnp.stack([real_part, imag_part], axis=-2).astype(jnp.bfloat16)
    weighted = weighted.reshape(op_count, row_count, 2 * mode_count)
    chosen = jnp.take(stacked[:, 0], directions, axis=0, mode="clip")
    blocks = jnp.einsum("ork,orm->okm", weighted, chosen, preferred_element_type=jnp.float32)
    field_real = blocks[:, :mode_count, :mode_count] - blocks[:, mode_count:, mode_count:]
    field_imag = blocks[:, :mode_count, mode_count:] + blocks[:, mode_count:, :mode_count]
    partial_sum = jnp.concatenate([field_real, field_imag], axis=-1)[None]
    flat_sum = partial_sum.reshape(-1, partial_sum.shape[-1])
    digits = radix_digits("gy") + radix_digits("gx")
    reduced = digit_sum(flat_sum, digits)
    other_part = lax.ppermute(reduced, "ta", [(0, 1), (1, 0)])
    both_parts = jnp.where(
        lax.axis_index("ta") == 0,
        jnp.stack([reduced, other_part]),
        jnp.stack([other_part, reduced]),
    )
    whole_field = (digit_gather(both_parts, digits) * scale_norm).reshape(
        (2,) + partial_sum.shape[1:]
    )
    own_fields = lax.dynamic_index_in_dim(whole_field, lax.axis_index("ta"), 0, keepdims=True)
    highest = lax.Precision.HIGHEST
    sink_field = jnp.take(whole_field, pairs[:, 0], axis=0, mode="clip")
    source_field = jnp.take(whole_field, pairs[:, 1], axis=0, mode="clip")
    prop_real = perambulators[..., :mode_count]
    prop_imag = perambulators[..., mode_count:]
    prop_block = jnp.concatenate(
        [perambulators, jnp.concatenate([-prop_imag, prop_real], axis=-1)], axis=-2
    )
    left_product = jnp.einsum("poik,pkj->poij", sink_field, prop_block, precision=highest)
    source_block = jnp.concatenate(
        [
            source_field,
            jnp.concatenate(
                [-source_field[..., mode_count:], source_field[..., :mode_count]], axis=-1
            ),
        ],
        axis=-2,
    )
    right_product = jnp.einsum("pik,pokj->poij", perambulators, source_block, precision=highest)
    correlator = jnp.einsum("paij,pbij->pab", left_product, right_product, precision=highest)
    correlator = (correlator / (mode_count * mode_count)).reshape(
        pairs.shape[0], op_count * op_count
    )
    return (own_fields, correlator)


def solution(mesh):
    in_specs = (
        P("ta", "gx", "gy", None, None, None),
        P("ta", "gx", "gy", None, None, None, None),
        P(),
        P(),
        P(("gx", "gy", "ta"), None),
        P(("gx", "gy", "ta"), None, None),
    )
    out_specs = (P("ta", None, None, None), P(("gx", "gy", "ta"), None))
    return jax.shard_map(local, mesh=mesh, in_specs=in_specs, out_specs=out_specs, check_vma=False)
```

```python
import math

import jax
import jax.numpy as jnp
from jax import lax
from jax.sharding import PartitionSpec as P


def from_behind(value, axis, steps):
    count = lax.axis_size(axis)
    pairs = [(source, (source + steps) % count) for source in range(count)]
    return lax.ppermute(value, axis, pairs)


def partner_pairs(axis, mask):
    return [(index, index ^ mask) for index in range(lax.axis_size(axis))]


def radix_digits(axis):
    bits = lax.axis_size(axis).bit_length() - 1
    widths = [1] * (bits % 2) + [2] * (bits // 2)
    lows = [sum(widths[:n]) for n in range(len(widths))]
    return [(axis, low, width) for low, width in zip(lows, widths)]


def digit_sum(value, digits):
    for axis, low, width in digits:
        count = 1 << width
        digit = (lax.axis_index(axis) >> low) & (count - 1)
        part = value.shape[0] // count
        total = lax.dynamic_slice_in_dim(value, digit * part, part, 0)
        for shift in range(1, count):
            send = lax.dynamic_slice_in_dim(value, (digit ^ shift) * part, part, 0)
            total = total + lax.ppermute(send, axis, partner_pairs(axis, shift << low))
        value = total
    return value


def digit_gather(value, digits):
    for axis, low, width in reversed(digits):
        count = 1 << width
        digit = (lax.axis_index(axis) >> low) & (count - 1)
        got = [value] + [
            lax.ppermute(value, axis, partner_pairs(axis, shift << low)) for shift in range(1, count)
        ]
        pieces = []
        for place in range(count):
            piece = got[0]
            for shift in range(1, count):
                piece = jnp.where((place ^ digit) == shift, got[shift], piece)
            pieces.append(piece)
        value = jnp.concatenate(pieces, 1)
    return value

def link_parts(raw_links):
    slice_count, wide_x, wide_y = (raw_links.shape[0], raw_links.shape[1], raw_links.shape[2])
    z_count = raw_links.shape[-1] // 2
    split = raw_links.reshape(slice_count, wide_x, wide_y, 3, 3, 3, 2, z_count)
    moved = jnp.transpose(split, (3, 6, 0, 1, 2, 7, 4, 5))
    return (moved[:, 0], moved[:, 1])


def color_apply(real_links, imag_links, vectors, dagger):
    pattern = "...ba,...bpk->...apk" if dagger else "...ab,...bpk->...apk"
    real_term = jnp.einsum(pattern, real_links, vectors, preferred_element_type=jnp.float32)
    imag_term = jnp.einsum(pattern, imag_links, vectors, preferred_element_type=jnp.float32)
    if dagger:
        imag_term = -imag_term
    real_out = real_term[..., 0, :] - imag_term[..., 1, :]
    imag_out = real_term[..., 1, :] + imag_term[..., 0, :]
    return jnp.stack([real_out, imag_out], axis=-2)


def phase_parts(momentum, coord_x, coord_y, coord_z, span_x, span_y, span_z):
    fraction = (jnp.mod(momentum[0] * coord_x, span_x).astype(jnp.float32) / span_x)[:, None, None]
    fraction = (
        fraction
        + (jnp.mod(momentum[1] * coord_y, span_y).astype(jnp.float32) / span_y)[None, :, None]
    )
    fraction = (
        fraction
        + (jnp.mod(momentum[2] * coord_z, span_z).astype(jnp.float32) / span_z)[None, None, :]
    )
    phase_angle = 2.0 * math.pi * fraction
    return (jnp.cos(phase_angle)[..., None, None], jnp.sin(phase_angle)[..., None, None])


def complex_product(left_side, right_side):
    half_width = left_side.shape[-2]
    highest = lax.Precision.HIGHEST
    left_real, left_imag = (left_side[..., :half_width], left_side[..., half_width:])
    right_real, right_imag = (right_side[..., :half_width], right_side[..., half_width:])
    real_out = jnp.matmul(left_real, right_real, precision=highest) - jnp.matmul(
        left_imag, right_imag, precision=highest
    )
    imag_out = jnp.matmul(left_real, right_imag, precision=highest) + jnp.matmul(
        left_imag, right_real, precision=highest
    )
    return jnp.concatenate([real_out, imag_out], axis=-1)


def local(eigvecs, links, momenta, directions, pairs, perambulators):
    slices, cells_x, cells_y, cells_z = (
        eigvecs.shape[0],
        eigvecs.shape[1],
        eigvecs.shape[2],
        eigvecs.shape[3],
    )
    mode_count = eigvecs.shape[-1] // 2
    op_count = momenta.shape[0]
    span_x = cells_x * lax.axis_size("gx")
    span_y = cells_y * lax.axis_size("gy")
    scale_norm = 1.0 / math.sqrt(3 * span_x * span_y * cells_z)
    vectors = eigvecs.reshape(slices, cells_x, cells_y, cells_z, 3, 2, mode_count)
    real_links, imag_links = link_parts(links)
    ahead_x = from_behind(eigvecs, "gx", -1)
    next_x = jnp.concatenate(
        [vectors[:, 1:], ahead_x.reshape(slices, 1, cells_y, cells_z, 3, 2, mode_count)], axis=1
    )
    back_x = color_apply(real_links[0], imag_links[0], vectors, True).astype(jnp.bfloat16)
    behind_x = from_behind(back_x, "gx", 1)
    prev_x = jnp.concatenate([behind_x, back_x[:, :-1]], axis=1)
    ahead_y = from_behind(eigvecs[:, :, :1], "gy", -1)
    next_y = jnp.concatenate(
        [vectors[:, :, 1:], ahead_y.reshape(slices, cells_x, 1, cells_z, 3, 2, mode_count)], axis=2
    )
    back_y = color_apply(real_links[1], imag_links[1], vectors, True).astype(jnp.bfloat16)
    behind_y = from_behind(back_y[:, :, -1:], "gy", 1)
    prev_y = jnp.concatenate([behind_y, back_y[:, :, :-1]], axis=2)
    forward_x = color_apply(real_links[0], imag_links[0], next_x, False)
    displaced_x = (forward_x - prev_x).astype(jnp.bfloat16)
    forward_y = color_apply(real_links[1], imag_links[1], next_y, False)
    displaced_y = (forward_y - prev_y).astype(jnp.bfloat16)
    forward_z = color_apply(real_links[2], imag_links[2], jnp.roll(vectors, -1, axis=3), False)
    back_z = color_apply(real_links[2], imag_links[2], vectors, True).astype(jnp.bfloat16)
    displaced_z = (forward_z - jnp.roll(back_z, 1, axis=3)).astype(jnp.bfloat16)
    row_count = cells_x * cells_y * cells_z * 3
    stacked = jnp.stack([displaced_x, displaced_y, displaced_z]).reshape(
        3, slices, row_count, 2 * mode_count
    )
    coord_x = lax.axis_index("gx") * cells_x + jnp.arange(cells_x, dtype=jnp.int32)
    coord_y = lax.axis_index("gy") * cells_y + jnp.arange(cells_y, dtype=jnp.int32)
    coord_z = jnp.arange(cells_z, dtype=jnp.int32)
    cosine, sine_part = jax.vmap(
        lambda momentum: phase_parts(momentum, coord_x, coord_y, coord_z, span_x, span_y, cells_z)
    )(momenta)
    row_shape = (op_count, cells_x, cells_y, cells_z, 3, 1)
    row_cosine = jnp.broadcast_to(cosine[..., :1, :], row_shape).reshape(op_count, row_count, 1)
    row_sine = jnp.broadcast_to(sine_part[..., :1, :], row_shape).reshape(op_count, row_count, 1)
    vec_rows = eigvecs.reshape(row_count, 2 * mode_count)
    vec_real = vec_rows[:, :mode_count]
    vec_imag = vec_rows[:, mode_count:]
    cosine_side = jnp.concatenate([vec_real, -vec_imag], axis=-1).astype(jnp.float32)
    sine_side = jnp.concatenate([-vec_imag, -vec_real], axis=-1).astype(jnp.float32)
    weighted = (row_cosine * cosine_side[None] + row_sine * sine_side[None]).astype(jnp.bfloat16)
    chosen = jnp.take(stacked[:, 0], directions, axis=0, mode="clip")
    blocks = jnp.einsum("ork,orm->okm", weighted, chosen, preferred_element_type=jnp.float32)
    field_real = blocks[:, :mode_count, :mode_count] - blocks[:, mode_count:, mode_count:]
    field_imag = blocks[:, :mode_count, mode_count:] + blocks[:, mode_count:, :mode_count]
    partial_sum = jnp.concatenate([field_real, field_imag], axis=-1)[None]
    flat_sum = partial_sum.reshape(-1, partial_sum.shape[-1])
    digits = radix_digits("gy") + radix_digits("gx")
    reduced = digit_sum(flat_sum, digits)
    other_part = lax.ppermute(reduced, "ta", [(0, 1), (1, 0)])
    both_parts = jnp.where(
        lax.axis_index("ta") == 0,
        jnp.stack([reduced, other_part]),
        jnp.stack([other_part, reduced]),
    )
    whole_field = (digit_gather(both_parts, digits) * scale_norm).reshape(
        (2,) + partial_sum.shape[1:]
    )
    own_fields = lax.dynamic_index_in_dim(whole_field, lax.axis_index("ta"), 0, keepdims=True)
    highest = lax.Precision.HIGHEST
    sink_field = jnp.take(whole_field, pairs[:, 0], axis=0, mode="clip")
    source_field = jnp.take(whole_field, pairs[:, 1], axis=0, mode="clip")
    prop_real = perambulators[..., :mode_count]
    prop_imag = perambulators[..., mode_count:]
    prop_block = jnp.concatenate(
        [perambulators, jnp.concatenate([-prop_imag, prop_real], axis=-1)], axis=-2
    )
    left_product = jnp.einsum("poik,pkj->poij", sink_field, prop_block, precision=highest)
    source_block = jnp.concatenate(
        [
            source_field,
            jnp.concatenate(
                [-source_field[..., mode_count:], source_field[..., :mode_count]], axis=-1
            ),
        ],
        axis=-2,
    )
    right_product = jnp.einsum("pik,pokj->poij", perambulators, source_block, precision=highest)
    correlator = jnp.einsum("paij,pbij->pab", left_product, right_product, precision=highest)
    correlator = (correlator / (mode_count * mode_count)).reshape(
        pairs.shape[0], op_count * op_count
    )
    return (own_fields, correlator)


def solution(mesh):
    in_specs = (
        P("ta", "gx", "gy", None, None, None),
        P("ta", "gx", "gy", None, None, None, None),
        P(),
        P(),
        P(("gx", "gy", "ta"), None),
        P(("gx", "gy", "ta"), None, None),
    )
    out_specs = (P("ta", None, None, None), P(("gx", "gy", "ta"), None))
    return jax.shard_map(local, mesh=mesh, in_specs=in_specs, out_specs=out_specs, check_vma=False)
```

```python
import math

import jax
import jax.numpy as jnp
from jax import lax
from jax.sharding import PartitionSpec as P


def from_behind(value, axis, steps):
    count = lax.axis_size(axis)
    pairs = [(source, (source + steps) % count) for source in range(count)]
    return lax.ppermute(value, axis, pairs)


def partner_pairs(axis, mask):
    return [(index, index ^ mask) for index in range(lax.axis_size(axis))]


def radix_digits(axis):
    bits = lax.axis_size(axis).bit_length() - 1
    widths = [1] * (bits % 2) + [2] * (bits // 2)
    lows = [sum(widths[:n]) for n in range(len(widths))]
    return [(axis, low, width) for low, width in zip(lows, widths)]


def digit_sum(value, digits):
    for axis, low, width in digits:
        count = 1 << width
        digit = (lax.axis_index(axis) >> low) & (count - 1)
        part = value.shape[0] // count
        total = lax.dynamic_slice_in_dim(value, digit * part, part, 0)
        for shift in range(1, count):
            send = lax.dynamic_slice_in_dim(value, (digit ^ shift) * part, part, 0)
            total = total + lax.ppermute(send, axis, partner_pairs(axis, shift << low))
        value = total
    return value


def digit_gather(value, digits):
    for axis, low, width in reversed(digits):
        count = 1 << width
        digit = (lax.axis_index(axis) >> low) & (count - 1)
        got = [value] + [
            lax.ppermute(value, axis, partner_pairs(axis, shift << low)) for shift in range(1, count)
        ]
        pieces = []
        for place in range(count):
            piece = got[0]
            for shift in range(1, count):
                piece = jnp.where((place ^ digit) == shift, got[shift], piece)
            pieces.append(piece)
        value = jnp.concatenate(pieces, 1)
    return value

def link_parts(raw_links):
    slice_count, wide_x, wide_y = (raw_links.shape[0], raw_links.shape[1], raw_links.shape[2])
    z_count = raw_links.shape[-1] // 2
    split = raw_links.reshape(slice_count, wide_x, wide_y, 3, 3, 3, 2, z_count)
    moved = jnp.transpose(split, (3, 6, 0, 1, 2, 7, 4, 5))
    return (moved[:, 0], moved[:, 1])


def color_apply(real_links, imag_links, vectors, dagger):
    pattern = "...ba,...bpk->...apk" if dagger else "...ab,...bpk->...apk"
    real_term = jnp.einsum(pattern, real_links, vectors, preferred_element_type=jnp.float32)
    imag_term = jnp.einsum(pattern, imag_links, vectors, preferred_element_type=jnp.float32)
    if dagger:
        imag_term = -imag_term
    real_out = real_term[..., 0, :] - imag_term[..., 1, :]
    imag_out = real_term[..., 1, :] + imag_term[..., 0, :]
    return jnp.stack([real_out, imag_out], axis=-2)


def phase_parts(momentum, coord_x, coord_y, coord_z, span_x, span_y, span_z):
    fraction = (jnp.mod(momentum[0] * coord_x, span_x).astype(jnp.float32) / span_x)[:, None, None]
    fraction = (
        fraction
        + (jnp.mod(momentum[1] * coord_y, span_y).astype(jnp.float32) / span_y)[None, :, None]
    )
    fraction = (
        fraction
        + (jnp.mod(momentum[2] * coord_z, span_z).astype(jnp.float32) / span_z)[None, None, :]
    )
    phase_angle = 2.0 * math.pi * fraction
    return (jnp.cos(phase_angle)[..., None, None], jnp.sin(phase_angle)[..., None, None])


def complex_product(left_side, right_side):
    half_width = left_side.shape[-2]
    highest = lax.Precision.HIGHEST
    left_real, left_imag = (left_side[..., :half_width], left_side[..., half_width:])
    right_real, right_imag = (right_side[..., :half_width], right_side[..., half_width:])
    real_out = jnp.matmul(left_real, right_real, precision=highest) - jnp.matmul(
        left_imag, right_imag, precision=highest
    )
    imag_out = jnp.matmul(left_real, right_imag, precision=highest) + jnp.matmul(
        left_imag, right_real, precision=highest
    )
    return jnp.concatenate([real_out, imag_out], axis=-1)


def local(eigvecs, links, momenta, directions, pairs, perambulators):
    slices, cells_x, cells_y, cells_z = (
        eigvecs.shape[0],
        eigvecs.shape[1],
        eigvecs.shape[2],
        eigvecs.shape[3],
    )
    mode_count = eigvecs.shape[-1] // 2
    op_count = momenta.shape[0]
    span_x = cells_x * lax.axis_size("gx")
    span_y = cells_y * lax.axis_size("gy")
    scale_norm = 1.0 / math.sqrt(3 * span_x * span_y * cells_z)
    planes = jnp.transpose(eigvecs[0], (0, 1, 3, 2, 4))
    vec_wide = planes.astype(jnp.float32)
    link_wide = jnp.transpose(
        links[0].reshape(cells_x, cells_y, 3, 3, 3, 2, cells_z), (2, 5, 0, 1, 3, 4, 6)
    ).astype(jnp.float32)
    row_count = cells_x * cells_y * cells_z * 3

    def colour_apply(direction, vectors, dagger):
        real_links, imag_links = (link_wide[direction, 0], link_wide[direction, 1])
        if dagger:
            real_links = jnp.swapaxes(real_links, 2, 3)
            imag_links = jnp.swapaxes(imag_links, 2, 3)
        real_term = sum(real_links[:, :, :, b, :, None] * vectors[:, :, None, b] for b in range(3))
        imag_term = sum(imag_links[:, :, :, b, :, None] * vectors[:, :, None, b] for b in range(3))
        if dagger:
            imag_term = -imag_term
        turned = jnp.concatenate([-imag_term[..., mode_count:], imag_term[..., :mode_count]], -1)
        return real_term + turned

    ahead_x = from_behind(planes[:1], "gx", -1).astype(jnp.float32)
    next_x = jnp.concatenate([vec_wide[1:], ahead_x], axis=0)
    back_x = colour_apply(0, vec_wide, True).astype(jnp.bfloat16)
    prev_x = jnp.concatenate([from_behind(back_x[-1:], "gx", 1), back_x[:-1]], axis=0)
    ahead_y = from_behind(planes[:, :1], "gy", -1).astype(jnp.float32)
    next_y = jnp.concatenate([vec_wide[:, 1:], ahead_y], axis=1)
    back_y = colour_apply(1, vec_wide, True).astype(jnp.bfloat16)
    prev_y = jnp.concatenate([from_behind(back_y[:, -1:], "gy", 1), back_y[:, :-1]], axis=1)
    back_z = colour_apply(2, vec_wide, True).astype(jnp.bfloat16)
    prev_z = jnp.roll(back_z, 1, axis=3)
    displaced = [
        (colour_apply(0, next_x, False) - prev_x.astype(jnp.float32)).astype(jnp.bfloat16),
        (colour_apply(1, next_y, False) - prev_y.astype(jnp.float32)).astype(jnp.bfloat16),
        (colour_apply(2, jnp.roll(vec_wide, -1, axis=3), False) - prev_z.astype(jnp.float32)).astype(
            jnp.bfloat16
        ),
    ]
    stacked = jnp.stack(displaced).reshape(3, row_count, 2 * mode_count)
    coord_x = lax.axis_index("gx") * cells_x + jnp.arange(cells_x, dtype=jnp.int32)
    coord_y = lax.axis_index("gy") * cells_y + jnp.arange(cells_y, dtype=jnp.int32)
    coord_z = jnp.arange(cells_z, dtype=jnp.int32)
    cosine, sine_part = jax.vmap(
        lambda momentum: phase_parts(momentum, coord_x, coord_y, coord_z, span_x, span_y, cells_z)
    )(momenta)
    row_shape = (op_count, cells_x, cells_y, 3, cells_z, 1)
    site_shape = (op_count, cells_x, cells_y, 1, cells_z, 1)
    row_cosine = jnp.broadcast_to(cosine.reshape(site_shape), row_shape).reshape(op_count, row_count, 1)
    row_sine = jnp.broadcast_to(sine_part.reshape(site_shape), row_shape).reshape(op_count, row_count, 1)
    vec_rows = planes.reshape(row_count, 2 * mode_count)
    vec_real = vec_rows[:, :mode_count]
    vec_imag = vec_rows[:, mode_count:]
    cosine_side = jnp.concatenate([vec_real, -vec_imag], axis=-1).astype(jnp.float32)
    sine_side = jnp.concatenate([-vec_imag, -vec_real], axis=-1).astype(jnp.float32)
    weighted = (row_cosine * cosine_side[None] + row_sine * sine_side[None]).astype(jnp.bfloat16)
    chosen = jnp.take(stacked, directions, axis=0, mode="clip")
    blocks = jnp.einsum("ork,orm->okm", weighted, chosen, preferred_element_type=jnp.float32)
    field_real = blocks[:, :mode_count, :mode_count] - blocks[:, mode_count:, mode_count:]
    field_imag = blocks[:, :mode_count, mode_count:] + blocks[:, mode_count:, :mode_count]
    partial_sum = jnp.concatenate([field_real, field_imag], axis=-1)[None]
    flat_sum = partial_sum.reshape(-1, partial_sum.shape[-1])
    digits = radix_digits("gy") + radix_digits("gx")
    reduced = digit_sum(flat_sum, digits)
    other_part = lax.ppermute(reduced, "ta", [(0, 1), (1, 0)])
    both_parts = jnp.where(
        lax.axis_index("ta") == 0,
        jnp.stack([reduced, other_part]),
        jnp.stack([other_part, reduced]),
    )
    whole_field = (digit_gather(both_parts, digits) * scale_norm).reshape(
        (2,) + partial_sum.shape[1:]
    )
    own_fields = lax.dynamic_index_in_dim(whole_field, lax.axis_index("ta"), 0, keepdims=True)
    highest = lax.Precision.HIGHEST
    sink_field = jnp.take(whole_field, pairs[:, 0], axis=0, mode="clip")
    source_field = jnp.take(whole_field, pairs[:, 1], axis=0, mode="clip")
    prop_real = perambulators[..., :mode_count]
    prop_imag = perambulators[..., mode_count:]
    prop_block = jnp.concatenate(
        [perambulators, jnp.concatenate([-prop_imag, prop_real], axis=-1)], axis=-2
    )
    left_product = jnp.einsum("poik,pkj->poij", sink_field, prop_block, precision=highest)
    source_block = jnp.concatenate(
        [
            source_field,
            jnp.concatenate(
                [-source_field[..., mode_count:], source_field[..., :mode_count]], axis=-1
            ),
        ],
        axis=-2,
    )
    right_product = jnp.einsum("pik,pokj->poij", perambulators, source_block, precision=highest)
    correlator = jnp.einsum("paij,pbij->pab", left_product, right_product, precision=highest)
    correlator = (correlator / (mode_count * mode_count)).reshape(
        pairs.shape[0], op_count * op_count
    )
    return (own_fields, correlator)


def solution(mesh):
    in_specs = (
        P("ta", "gx", "gy", None, None, None),
        P("ta", "gx", "gy", None, None, None, None),
        P(),
        P(),
        P(("gx", "gy", "ta"), None),
        P(("gx", "gy", "ta"), None, None),
    )
    out_specs = (P("ta", None, None, None), P(("gx", "gy", "ta"), None))
    return jax.shard_map(local, mesh=mesh, in_specs=in_specs, out_specs=out_specs, check_vma=False)
```

```python
import math

import jax
import jax.numpy as jnp
from jax import lax
from jax.sharding import PartitionSpec as P


def from_behind(value, axis, steps):
    count = lax.axis_size(axis)
    pairs = [(source, (source + steps) % count) for source in range(count)]
    return lax.ppermute(value, axis, pairs)


def partner_pairs(axis, mask):
    return [(index, index ^ mask) for index in range(lax.axis_size(axis))]


def radix_digits(axis):
    bits = lax.axis_size(axis).bit_length() - 1
    widths = [1] * (bits % 2) + [2] * (bits // 2)
    lows = [sum(widths[:n]) for n in range(len(widths))]
    return [(axis, low, width) for low, width in zip(lows, widths)]


def digit_sum(value, digits):
    for axis, low, width in digits:
        count = 1 << width
        digit = (lax.axis_index(axis) >> low) & (count - 1)
        part = value.shape[0] // count
        total = lax.dynamic_slice_in_dim(value, digit * part, part, 0)
        for shift in range(1, count):
            send = lax.dynamic_slice_in_dim(value, (digit ^ shift) * part, part, 0)
            total = total + lax.ppermute(send, axis, partner_pairs(axis, shift << low))
        value = total
    return value


def digit_gather(value, digits):
    for axis, low, width in reversed(digits):
        count = 1 << width
        digit = (lax.axis_index(axis) >> low) & (count - 1)
        got = [value] + [
            lax.ppermute(value, axis, partner_pairs(axis, shift << low)) for shift in range(1, count)
        ]
        pieces = []
        for place in range(count):
            piece = got[0]
            for shift in range(1, count):
                piece = jnp.where((place ^ digit) == shift, got[shift], piece)
            pieces.append(piece)
        value = jnp.concatenate(pieces, 1)
    return value

def phase_parts(momentum, coord_x, coord_y, coord_z, span_x, span_y, span_z):
    fraction = (jnp.mod(momentum[0] * coord_x, span_x).astype(jnp.float32) / span_x)[:, None, None]
    fraction = (
        fraction
        + (jnp.mod(momentum[1] * coord_y, span_y).astype(jnp.float32) / span_y)[None, :, None]
    )
    fraction = (
        fraction
        + (jnp.mod(momentum[2] * coord_z, span_z).astype(jnp.float32) / span_z)[None, None, :]
    )
    phase_angle = 2.0 * math.pi * fraction
    return (jnp.cos(phase_angle)[..., None, None], jnp.sin(phase_angle)[..., None, None])


def local(eigvecs, links, momenta, directions, pairs, perambulators):
    slices, cells_x, cells_y, cells_z = (
        eigvecs.shape[0],
        eigvecs.shape[1],
        eigvecs.shape[2],
        eigvecs.shape[3],
    )
    mode_count = eigvecs.shape[-1] // 2
    op_count = momenta.shape[0]
    span_x = cells_x * lax.axis_size("gx")
    span_y = cells_y * lax.axis_size("gy")
    scale_norm = 1.0 / math.sqrt(3 * span_x * span_y * cells_z)
    planes = jnp.transpose(eigvecs[0], (0, 1, 3, 2, 4))
    vec_wide = planes.astype(jnp.float32)
    link_wide = jnp.transpose(
        links[0].reshape(cells_x, cells_y, 3, 3, 3, 2, cells_z), (2, 5, 0, 1, 3, 4, 6)
    ).astype(jnp.float32)
    row_count = cells_x * cells_y * cells_z * 3

    def colour_apply(direction, vectors, dagger):
        real_links, imag_links = (link_wide[direction, 0], link_wide[direction, 1])
        if dagger:
            real_links = jnp.swapaxes(real_links, 2, 3)
            imag_links = jnp.swapaxes(imag_links, 2, 3)
        real_term = sum(real_links[:, :, :, b, :, None] * vectors[:, :, None, b] for b in range(3))
        imag_term = sum(imag_links[:, :, :, b, :, None] * vectors[:, :, None, b] for b in range(3))
        if dagger:
            imag_term = -imag_term
        turned = jnp.concatenate([-imag_term[..., mode_count:], imag_term[..., :mode_count]], -1)
        return real_term + turned

    ahead_x = from_behind(planes[:1], "gx", -1).astype(jnp.float32)
    next_x = jnp.concatenate([vec_wide[1:], ahead_x], axis=0)
    back_x = colour_apply(0, vec_wide, True).astype(jnp.bfloat16)
    prev_x = jnp.concatenate([from_behind(back_x[-1:], "gx", 1), back_x[:-1]], axis=0)
    ahead_y = from_behind(planes[:, :1], "gy", -1).astype(jnp.float32)
    next_y = jnp.concatenate([vec_wide[:, 1:], ahead_y], axis=1)
    back_y = colour_apply(1, vec_wide, True).astype(jnp.bfloat16)
    prev_y = jnp.concatenate([from_behind(back_y[:, -1:], "gy", 1), back_y[:, :-1]], axis=1)
    back_z = colour_apply(2, vec_wide, True).astype(jnp.bfloat16)
    prev_z = jnp.roll(back_z, 1, axis=3)
    displaced = [
        (colour_apply(0, next_x, False) - prev_x.astype(jnp.float32)).astype(jnp.bfloat16),
        (colour_apply(1, next_y, False) - prev_y.astype(jnp.float32)).astype(jnp.bfloat16),
        (colour_apply(2, jnp.roll(vec_wide, -1, axis=3), False) - prev_z.astype(jnp.float32)).astype(
            jnp.bfloat16
        ),
    ]
    stacked = jnp.stack(displaced).reshape(3, row_count, 2 * mode_count)
    coord_x = lax.axis_index("gx") * cells_x + jnp.arange(cells_x, dtype=jnp.int32)
    coord_y = lax.axis_index("gy") * cells_y + jnp.arange(cells_y, dtype=jnp.int32)
    coord_z = jnp.arange(cells_z, dtype=jnp.int32)
    cosine, sine_part = jax.vmap(
        lambda momentum: phase_parts(momentum, coord_x, coord_y, coord_z, span_x, span_y, cells_z)
    )(momenta)
    row_shape = (op_count, cells_x, cells_y, 3, cells_z, 1)
    site_shape = (op_count, cells_x, cells_y, 1, cells_z, 1)
    row_cosine = jnp.broadcast_to(cosine.reshape(site_shape), row_shape).reshape(op_count, row_count, 1)
    row_sine = jnp.broadcast_to(sine_part.reshape(site_shape), row_shape).reshape(op_count, row_count, 1)
    vec_rows = planes.reshape(row_count, 2 * mode_count)
    vec_real = vec_rows[:, :mode_count]
    vec_imag = vec_rows[:, mode_count:]
    cosine_side = jnp.concatenate([vec_real, -vec_imag], axis=-1).astype(jnp.float32)
    sine_side = jnp.concatenate([-vec_imag, -vec_real], axis=-1).astype(jnp.float32)
    weighted = (row_cosine * cosine_side[None] + row_sine * sine_side[None]).astype(jnp.bfloat16)
    chosen = jnp.take(stacked, directions, axis=0, mode="clip")
    blocks = jnp.einsum("ork,orm->okm", weighted, chosen, preferred_element_type=jnp.float32)
    field_real = blocks[:, :mode_count, :mode_count] - blocks[:, mode_count:, mode_count:]
    field_imag = blocks[:, :mode_count, mode_count:] + blocks[:, mode_count:, :mode_count]
    partial_sum = jnp.concatenate([field_real, field_imag], axis=-1)[None]
    flat_sum = partial_sum.reshape(-1, partial_sum.shape[-1])
    digits = radix_digits("gy") + radix_digits("gx")
    reduced = digit_sum(flat_sum, digits)
    other_part = lax.ppermute(reduced, "ta", [(0, 1), (1, 0)])
    both_parts = jnp.where(
        lax.axis_index("ta") == 0,
        jnp.stack([reduced, other_part]),
        jnp.stack([other_part, reduced]),
    )
    whole_field = (digit_gather(both_parts, digits) * scale_norm).reshape(
        (2,) + partial_sum.shape[1:]
    )
    own_fields = lax.dynamic_index_in_dim(whole_field, lax.axis_index("ta"), 0, keepdims=True)
    highest = lax.Precision.HIGHEST
    sink_field = whole_field[0][None]
    source_field = whole_field[0][None]
    for slot in range(1, whole_field.shape[0]):
        sink_field = jnp.where((pairs[:, 0] >= slot)[:, None, None, None], whole_field[slot][None], sink_field)
        source_field = jnp.where(
            (pairs[:, 1] >= slot)[:, None, None, None], whole_field[slot][None], source_field
        )
    prop_real = perambulators[..., :mode_count]
    prop_imag = perambulators[..., mode_count:]
    prop_block = jnp.concatenate(
        [perambulators, jnp.concatenate([-prop_imag, prop_real], axis=-1)], axis=-2
    )
    left_product = jnp.einsum("poik,pkj->poij", sink_field, prop_block, precision=highest)
    source_block = jnp.concatenate(
        [
            source_field,
            jnp.concatenate(
                [-source_field[..., mode_count:], source_field[..., :mode_count]], axis=-1
            ),
        ],
        axis=-2,
    )
    right_product = jnp.einsum("pik,pokj->poij", perambulators, source_block, precision=highest)
    correlator = jnp.einsum("paij,pbij->pab", left_product, right_product, precision=highest)
    correlator = (correlator / (mode_count * mode_count)).reshape(
        pairs.shape[0], op_count * op_count
    )
    return (own_fields, correlator)


def solution(mesh):
    in_specs = (
        P("ta", "gx", "gy", None, None, None),
        P("ta", "gx", "gy", None, None, None, None),
        P(),
        P(),
        P(("gx", "gy", "ta"), None),
        P(("gx", "gy", "ta"), None, None),
    )
    out_specs = (P("ta", None, None, None), P(("gx", "gy", "ta"), None))
    return jax.shard_map(local, mesh=mesh, in_specs=in_specs, out_specs=out_specs, check_vma=False)
```

```python
import math

import jax
import jax.numpy as jnp
from jax import lax
from jax.sharding import PartitionSpec as P


def from_behind(value, axis, steps):
    count = lax.axis_size(axis)
    pairs = [(source, (source + steps) % count) for source in range(count)]
    return lax.ppermute(value, axis, pairs)


def partner_pairs(axis, mask):
    return [(index, index ^ mask) for index in range(lax.axis_size(axis))]


def radix_digits(axis):
    bits = lax.axis_size(axis).bit_length() - 1
    widths = [1] * (bits % 2) + [2] * (bits // 2)
    lows = [sum(widths[:n]) for n in range(len(widths))]
    return [(axis, low, width) for low, width in zip(lows, widths)]


def digit_sum(value, digits):
    for axis, low, width in digits:
        count = 1 << width
        digit = (lax.axis_index(axis) >> low) & (count - 1)
        part = value.shape[0] // count
        total = lax.dynamic_slice_in_dim(value, digit * part, part, 0)
        for shift in range(1, count):
            send = lax.dynamic_slice_in_dim(value, (digit ^ shift) * part, part, 0)
            total = total + lax.ppermute(send, axis, partner_pairs(axis, shift << low))
        value = total
    return value


def digit_gather(value, digits):
    for axis, low, width in reversed(digits):
        count = 1 << width
        digit = (lax.axis_index(axis) >> low) & (count - 1)
        got = [value] + [
            lax.ppermute(value, axis, partner_pairs(axis, shift << low)) for shift in range(1, count)
        ]
        pieces = []
        for place in range(count):
            piece = got[0]
            for shift in range(1, count):
                piece = jnp.where((place ^ digit) == shift, got[shift], piece)
            pieces.append(piece)
        value = jnp.concatenate(pieces, 1)
    return value

def link_parts(raw_links):
    slice_count, wide_x, wide_y = (raw_links.shape[0], raw_links.shape[1], raw_links.shape[2])
    z_count = raw_links.shape[-1] // 2
    split = raw_links.reshape(slice_count, wide_x, wide_y, 3, 3, 3, 2, z_count)
    moved = jnp.transpose(split, (3, 6, 0, 1, 2, 7, 4, 5))
    return (moved[:, 0], moved[:, 1])


def color_apply(real_links, imag_links, vectors, dagger):
    pattern = "...ba,...bpk->...apk" if dagger else "...ab,...bpk->...apk"
    real_term = jnp.einsum(pattern, real_links, vectors, preferred_element_type=jnp.float32)
    imag_term = jnp.einsum(pattern, imag_links, vectors, preferred_element_type=jnp.float32)
    if dagger:
        imag_term = -imag_term
    real_out = real_term[..., 0, :] - imag_term[..., 1, :]
    imag_out = real_term[..., 1, :] + imag_term[..., 0, :]
    return jnp.stack([real_out, imag_out], axis=-2)


def phase_parts(momentum, coord_x, coord_y, coord_z, span_x, span_y, span_z):
    fraction = (jnp.mod(momentum[0] * coord_x, span_x).astype(jnp.float32) / span_x)[:, None, None]
    fraction = (
        fraction
        + (jnp.mod(momentum[1] * coord_y, span_y).astype(jnp.float32) / span_y)[None, :, None]
    )
    fraction = (
        fraction
        + (jnp.mod(momentum[2] * coord_z, span_z).astype(jnp.float32) / span_z)[None, None, :]
    )
    phase_angle = 2.0 * math.pi * fraction
    return (jnp.cos(phase_angle)[..., None, None], jnp.sin(phase_angle)[..., None, None])


def complex_product(left_side, right_side):
    half_width = left_side.shape[-2]
    highest = lax.Precision.HIGHEST
    left_real, left_imag = (left_side[..., :half_width], left_side[..., half_width:])
    right_real, right_imag = (right_side[..., :half_width], right_side[..., half_width:])
    real_out = jnp.matmul(left_real, right_real, precision=highest) - jnp.matmul(
        left_imag, right_imag, precision=highest
    )
    imag_out = jnp.matmul(left_real, right_imag, precision=highest) + jnp.matmul(
        left_imag, right_real, precision=highest
    )
    return jnp.concatenate([real_out, imag_out], axis=-1)


def local(eigvecs, links, momenta, directions, pairs, perambulators):
    slices, cells_x, cells_y, cells_z = (
        eigvecs.shape[0],
        eigvecs.shape[1],
        eigvecs.shape[2],
        eigvecs.shape[3],
    )
    mode_count = eigvecs.shape[-1] // 2
    op_count = momenta.shape[0]
    span_x = cells_x * lax.axis_size("gx")
    span_y = cells_y * lax.axis_size("gy")
    scale_norm = 1.0 / math.sqrt(3 * span_x * span_y * cells_z)
    planes = jnp.transpose(eigvecs[0], (0, 1, 3, 2, 4))
    vec_wide = planes.astype(jnp.float32)
    link_wide = jnp.transpose(
        links[0].reshape(cells_x, cells_y, 3, 3, 3, 2, cells_z), (2, 5, 0, 1, 3, 4, 6)
    ).astype(jnp.float32)
    row_count = cells_x * cells_y * cells_z * 3

    def colour_apply(direction, vectors, dagger):
        real_links, imag_links = (link_wide[direction, 0], link_wide[direction, 1])
        if dagger:
            real_links = jnp.swapaxes(real_links, 2, 3)
            imag_links = jnp.swapaxes(imag_links, 2, 3)
        real_term = sum(real_links[:, :, :, b, :, None] * vectors[:, :, None, b] for b in range(3))
        imag_term = sum(imag_links[:, :, :, b, :, None] * vectors[:, :, None, b] for b in range(3))
        if dagger:
            imag_term = -imag_term
        turned = jnp.concatenate([-imag_term[..., mode_count:], imag_term[..., :mode_count]], -1)
        return real_term + turned

    ahead_x = from_behind(planes[:1], "gx", -1).astype(jnp.float32)
    next_x = jnp.concatenate([vec_wide[1:], ahead_x], axis=0)
    back_x = colour_apply(0, vec_wide, True).astype(jnp.bfloat16)
    prev_x = jnp.concatenate([from_behind(back_x[-1:], "gx", 1), back_x[:-1]], axis=0)
    ahead_y = from_behind(planes[:, :1], "gy", -1).astype(jnp.float32)
    next_y = jnp.concatenate([vec_wide[:, 1:], ahead_y], axis=1)
    back_y = colour_apply(1, vec_wide, True).astype(jnp.bfloat16)
    prev_y = jnp.concatenate([from_behind(back_y[:, -1:], "gy", 1), back_y[:, :-1]], axis=1)
    back_z = colour_apply(2, vec_wide, True).astype(jnp.bfloat16)
    prev_z = jnp.roll(back_z, 1, axis=3)
    displaced = [
        (colour_apply(0, next_x, False) - prev_x.astype(jnp.float32)).astype(jnp.bfloat16),
        (colour_apply(1, next_y, False) - prev_y.astype(jnp.float32)).astype(jnp.bfloat16),
        (colour_apply(2, jnp.roll(vec_wide, -1, axis=3), False) - prev_z.astype(jnp.float32)).astype(
            jnp.bfloat16
        ),
    ]
    stacked = jnp.stack(displaced).reshape(3, row_count, 2 * mode_count)
    coord_x = lax.axis_index("gx") * cells_x + jnp.arange(cells_x, dtype=jnp.int32)
    coord_y = lax.axis_index("gy") * cells_y + jnp.arange(cells_y, dtype=jnp.int32)
    coord_z = jnp.arange(cells_z, dtype=jnp.int32)
    cosine, sine_part = jax.vmap(
        lambda momentum: phase_parts(momentum, coord_x, coord_y, coord_z, span_x, span_y, cells_z)
    )(momenta)
    row_shape = (op_count, cells_x, cells_y, 3, cells_z, 1)
    site_shape = (op_count, cells_x, cells_y, 1, cells_z, 1)
    row_cosine = jnp.broadcast_to(cosine.reshape(site_shape), row_shape).reshape(op_count, row_count, 1)
    row_sine = jnp.broadcast_to(sine_part.reshape(site_shape), row_shape).reshape(op_count, row_count, 1)
    vec_rows = planes.reshape(row_count, 2 * mode_count)
    vec_real = vec_rows[:, :mode_count]
    vec_imag = vec_rows[:, mode_count:]
    cosine_side = jnp.concatenate([vec_real, -vec_imag], axis=-1).astype(jnp.float32)
    sine_side = jnp.concatenate([-vec_imag, -vec_real], axis=-1).astype(jnp.float32)
    digits = radix_digits("gy") + radix_digits("gx")

    def field_part(start, length):
        part_cosine = lax.dynamic_slice_in_dim(row_cosine, start, length, 0)
        part_sine = lax.dynamic_slice_in_dim(row_sine, start, length, 0)
        weighted = (part_cosine * cosine_side[None] + part_sine * sine_side[None]).astype(jnp.bfloat16)
        part_directions = lax.dynamic_slice_in_dim(directions, start, length, 0)
        chosen = jnp.take(stacked, part_directions, axis=0, mode="clip")
        blocks = jnp.einsum("ork,orm->okm", weighted, chosen, preferred_element_type=jnp.float32)
        field_real = blocks[:, :mode_count, :mode_count] - blocks[:, mode_count:, mode_count:]
        field_imag = blocks[:, :mode_count, mode_count:] + blocks[:, mode_count:, :mode_count]
        return jnp.concatenate([field_real, field_imag], axis=-1).reshape(length * mode_count, -1)

    first_axis, first_low, first_width = digits[0]
    first_count = 1 << first_width
    share = op_count // first_count
    first_digit = (lax.axis_index(first_axis) >> first_low) & (first_count - 1)
    sent = [
        lax.ppermute(
            field_part((first_digit ^ shift) * share, share),
            first_axis,
            partner_pairs(first_axis, shift << first_low),
        )
        for shift in range(1, first_count)
    ]
    reduced = field_part(first_digit * share, share)
    for part in sent:
        reduced = reduced + part
    reduced = digit_sum(reduced, digits[1:])
    other_part = lax.ppermute(reduced, "ta", [(0, 1), (1, 0)])
    both_parts = jnp.where(
        lax.axis_index("ta") == 0,
        jnp.stack([reduced, other_part]),
        jnp.stack([other_part, reduced]),
    )
    whole_field = (digit_gather(both_parts, digits) * scale_norm).reshape(
        (2, op_count, mode_count, 2 * mode_count)
    )
    own_fields = lax.dynamic_index_in_dim(whole_field, lax.axis_index("ta"), 0, keepdims=True)
    highest = lax.Precision.HIGHEST
    sink_field = jnp.take(whole_field, pairs[:, 0], axis=0, mode="clip")
    source_field = jnp.take(whole_field, pairs[:, 1], axis=0, mode="clip")
    prop_real = perambulators[..., :mode_count]
    prop_imag = perambulators[..., mode_count:]
    prop_block = jnp.concatenate(
        [perambulators, jnp.concatenate([-prop_imag, prop_real], axis=-1)], axis=-2
    )
    left_product = jnp.einsum("poik,pkj->poij", sink_field, prop_block, precision=highest)
    source_block = jnp.concatenate(
        [
            source_field,
            jnp.concatenate(
                [-source_field[..., mode_count:], source_field[..., :mode_count]], axis=-1
            ),
        ],
        axis=-2,
    )
    right_product = jnp.einsum("pik,pokj->poij", perambulators, source_block, precision=highest)
    correlator = jnp.einsum("paij,pbij->pab", left_product, right_product, precision=highest)
    correlator = (correlator / (mode_count * mode_count)).reshape(
        pairs.shape[0], op_count * op_count
    )
    return (own_fields, correlator)


def solution(mesh):
    in_specs = (
        P("ta", "gx", "gy", None, None, None),
        P("ta", "gx", "gy", None, None, None, None),
        P(),
        P(),
        P(("gx", "gy", "ta"), None),
        P(("gx", "gy", "ta"), None, None),
    )
    out_specs = (P("ta", None, None, None), P(("gx", "gy", "ta"), None))
    return jax.shard_map(local, mesh=mesh, in_specs=in_specs, out_specs=out_specs, check_vma=False)
```

```python
import math

import jax
import jax.numpy as jnp
from jax import lax
from jax.sharding import PartitionSpec as P


def from_behind(value, axis, steps):
    count = lax.axis_size(axis)
    pairs = [(source, (source + steps) % count) for source in range(count)]
    return lax.ppermute(value, axis, pairs)


def partner_pairs(axis, mask):
    return [(index, index ^ mask) for index in range(lax.axis_size(axis))]


def radix_digits(axis):
    bits = lax.axis_size(axis).bit_length() - 1
    widths = [1] * (bits % 2) + [2] * (bits // 2)
    lows = [sum(widths[:n]) for n in range(len(widths))]
    return [(axis, low, width) for low, width in zip(lows, widths)]


def digit_sum(value, digits):
    for axis, low, width in digits:
        count = 1 << width
        digit = (lax.axis_index(axis) >> low) & (count - 1)
        part = value.shape[0] // count
        total = lax.dynamic_slice_in_dim(value, digit * part, part, 0)
        for shift in range(1, count):
            send = lax.dynamic_slice_in_dim(value, (digit ^ shift) * part, part, 0)
            total = total + lax.ppermute(send, axis, partner_pairs(axis, shift << low))
        value = total
    return value


def digit_gather(value, digits):
    for axis, low, width in reversed(digits):
        count = 1 << width
        digit = (lax.axis_index(axis) >> low) & (count - 1)
        got = [value] + [
            lax.ppermute(value, axis, partner_pairs(axis, shift << low)) for shift in range(1, count)
        ]
        part = value.shape[1]
        value = jnp.zeros(value.shape[:1] + (count * part,) + value.shape[2:], value.dtype)
        for shift in range(count):
            value = lax.dynamic_update_slice_in_dim(value, got[shift], (digit ^ shift) * part, 1)
    return value

def link_parts(raw_links):
    slice_count, wide_x, wide_y = (raw_links.shape[0], raw_links.shape[1], raw_links.shape[2])
    z_count = raw_links.shape[-1] // 2
    split = raw_links.reshape(slice_count, wide_x, wide_y, 3, 3, 3, 2, z_count)
    moved = jnp.transpose(split, (3, 6, 0, 1, 2, 7, 4, 5))
    return (moved[:, 0], moved[:, 1])


def color_apply(real_links, imag_links, vectors, dagger):
    pattern = "...ba,...bpk->...apk" if dagger else "...ab,...bpk->...apk"
    real_term = jnp.einsum(pattern, real_links, vectors, preferred_element_type=jnp.float32)
    imag_term = jnp.einsum(pattern, imag_links, vectors, preferred_element_type=jnp.float32)
    if dagger:
        imag_term = -imag_term
    real_out = real_term[..., 0, :] - imag_term[..., 1, :]
    imag_out = real_term[..., 1, :] + imag_term[..., 0, :]
    return jnp.stack([real_out, imag_out], axis=-2)


def phase_parts(momentum, coord_x, coord_y, coord_z, span_x, span_y, span_z):
    fraction = (jnp.mod(momentum[0] * coord_x, span_x).astype(jnp.float32) / span_x)[:, None, None]
    fraction = (
        fraction
        + (jnp.mod(momentum[1] * coord_y, span_y).astype(jnp.float32) / span_y)[None, :, None]
    )
    fraction = (
        fraction
        + (jnp.mod(momentum[2] * coord_z, span_z).astype(jnp.float32) / span_z)[None, None, :]
    )
    phase_angle = 2.0 * math.pi * fraction
    return (jnp.cos(phase_angle)[..., None, None], jnp.sin(phase_angle)[..., None, None])


def complex_product(left_side, right_side):
    half_width = left_side.shape[-2]
    highest = lax.Precision.HIGHEST
    left_real, left_imag = (left_side[..., :half_width], left_side[..., half_width:])
    right_real, right_imag = (right_side[..., :half_width], right_side[..., half_width:])
    real_out = jnp.matmul(left_real, right_real, precision=highest) - jnp.matmul(
        left_imag, right_imag, precision=highest
    )
    imag_out = jnp.matmul(left_real, right_imag, precision=highest) + jnp.matmul(
        left_imag, right_real, precision=highest
    )
    return jnp.concatenate([real_out, imag_out], axis=-1)


def local(eigvecs, links, momenta, directions, pairs, perambulators):
    slices, cells_x, cells_y, cells_z = (
        eigvecs.shape[0],
        eigvecs.shape[1],
        eigvecs.shape[2],
        eigvecs.shape[3],
    )
    mode_count = eigvecs.shape[-1] // 2
    op_count = momenta.shape[0]
    span_x = cells_x * lax.axis_size("gx")
    span_y = cells_y * lax.axis_size("gy")
    scale_norm = 1.0 / math.sqrt(3 * span_x * span_y * cells_z)
    planes = jnp.transpose(eigvecs[0], (0, 1, 3, 2, 4))
    vec_wide = planes.astype(jnp.float32)
    link_wide = jnp.transpose(
        links[0].reshape(cells_x, cells_y, 3, 3, 3, 2, cells_z), (2, 5, 0, 1, 3, 4, 6)
    ).astype(jnp.float32)
    row_count = cells_x * cells_y * cells_z * 3

    def colour_apply(direction, vectors, dagger):
        real_links, imag_links = (link_wide[direction, 0], link_wide[direction, 1])
        if dagger:
            real_links = jnp.swapaxes(real_links, 2, 3)
            imag_links = jnp.swapaxes(imag_links, 2, 3)
        real_term = sum(real_links[:, :, :, b, :, None] * vectors[:, :, None, b] for b in range(3))
        imag_term = sum(imag_links[:, :, :, b, :, None] * vectors[:, :, None, b] for b in range(3))
        if dagger:
            imag_term = -imag_term
        turned = jnp.concatenate([-imag_term[..., mode_count:], imag_term[..., :mode_count]], -1)
        return real_term + turned

    ahead_x = from_behind(planes[:1], "gx", -1).astype(jnp.float32)
    next_x = jnp.concatenate([vec_wide[1:], ahead_x], axis=0)
    back_x = colour_apply(0, vec_wide, True).astype(jnp.bfloat16)
    prev_x = jnp.concatenate([from_behind(back_x[-1:], "gx", 1), back_x[:-1]], axis=0)
    ahead_y = from_behind(planes[:, :1], "gy", -1).astype(jnp.float32)
    next_y = jnp.concatenate([vec_wide[:, 1:], ahead_y], axis=1)
    back_y = colour_apply(1, vec_wide, True).astype(jnp.bfloat16)
    prev_y = jnp.concatenate([from_behind(back_y[:, -1:], "gy", 1), back_y[:, :-1]], axis=1)
    back_z = colour_apply(2, vec_wide, True).astype(jnp.bfloat16)
    prev_z = jnp.roll(back_z, 1, axis=3)
    displaced = [
        (colour_apply(0, next_x, False) - prev_x.astype(jnp.float32)).astype(jnp.bfloat16),
        (colour_apply(1, next_y, False) - prev_y.astype(jnp.float32)).astype(jnp.bfloat16),
        (colour_apply(2, jnp.roll(vec_wide, -1, axis=3), False) - prev_z.astype(jnp.float32)).astype(
            jnp.bfloat16
        ),
    ]
    stacked = jnp.stack(displaced).reshape(3, row_count, 2 * mode_count)
    coord_x = lax.axis_index("gx") * cells_x + jnp.arange(cells_x, dtype=jnp.int32)
    coord_y = lax.axis_index("gy") * cells_y + jnp.arange(cells_y, dtype=jnp.int32)
    coord_z = jnp.arange(cells_z, dtype=jnp.int32)
    cosine, sine_part = jax.vmap(
        lambda momentum: phase_parts(momentum, coord_x, coord_y, coord_z, span_x, span_y, cells_z)
    )(momenta)
    row_shape = (op_count, cells_x, cells_y, 3, cells_z, 1)
    site_shape = (op_count, cells_x, cells_y, 1, cells_z, 1)
    row_cosine = jnp.broadcast_to(cosine.reshape(site_shape), row_shape).reshape(op_count, row_count, 1)
    row_sine = jnp.broadcast_to(sine_part.reshape(site_shape), row_shape).reshape(op_count, row_count, 1)
    vec_rows = planes.reshape(row_count, 2 * mode_count)
    vec_real = vec_rows[:, :mode_count]
    vec_imag = vec_rows[:, mode_count:]
    cosine_side = jnp.concatenate([vec_real, -vec_imag], axis=-1).astype(jnp.float32)
    sine_side = jnp.concatenate([-vec_imag, -vec_real], axis=-1).astype(jnp.float32)
    weighted = (row_cosine * cosine_side[None] + row_sine * sine_side[None]).astype(jnp.bfloat16)
    chosen = jnp.take(stacked, directions, axis=0, mode="clip")
    blocks = jnp.einsum("ork,orm->okm", weighted, chosen, preferred_element_type=jnp.float32)
    field_real = blocks[:, :mode_count, :mode_count] - blocks[:, mode_count:, mode_count:]
    field_imag = blocks[:, :mode_count, mode_count:] + blocks[:, mode_count:, :mode_count]
    partial_sum = jnp.concatenate([field_real, field_imag], axis=-1)[None]
    flat_sum = partial_sum.reshape(-1, partial_sum.shape[-1])
    digits = radix_digits("gy") + radix_digits("gx")
    reduced = digit_sum(flat_sum, digits)
    other_part = lax.ppermute(reduced, "ta", [(0, 1), (1, 0)])
    both_parts = jnp.where(
        lax.axis_index("ta") == 0,
        jnp.stack([reduced, other_part]),
        jnp.stack([other_part, reduced]),
    )
    whole_field = (digit_gather(both_parts, digits) * scale_norm).reshape(
        (2,) + partial_sum.shape[1:]
    )
    own_fields = lax.dynamic_index_in_dim(whole_field, lax.axis_index("ta"), 0, keepdims=True)
    highest = lax.Precision.HIGHEST
    sink_field = jnp.take(whole_field, pairs[:, 0], axis=0, mode="clip")
    source_field = jnp.take(whole_field, pairs[:, 1], axis=0, mode="clip")
    prop_real = perambulators[..., :mode_count]
    prop_imag = perambulators[..., mode_count:]
    prop_block = jnp.concatenate(
        [perambulators, jnp.concatenate([-prop_imag, prop_real], axis=-1)], axis=-2
    )
    left_product = jnp.einsum("poik,pkj->poij", sink_field, prop_block, precision=highest)
    source_block = jnp.concatenate(
        [
            source_field,
            jnp.concatenate(
                [-source_field[..., mode_count:], source_field[..., :mode_count]], axis=-1
            ),
        ],
        axis=-2,
    )
    right_product = jnp.einsum("pik,pokj->poij", perambulators, source_block, precision=highest)
    correlator = jnp.einsum("paij,pbij->pab", left_product, right_product, precision=highest)
    correlator = (correlator / (mode_count * mode_count)).reshape(
        pairs.shape[0], op_count * op_count
    )
    return (own_fields, correlator)


def solution(mesh):
    in_specs = (
        P("ta", "gx", "gy", None, None, None),
        P("ta", "gx", "gy", None, None, None, None),
        P(),
        P(),
        P(("gx", "gy", "ta"), None),
        P(("gx", "gy", "ta"), None, None),
    )
    out_specs = (P("ta", None, None, None), P(("gx", "gy", "ta"), None))
    return jax.shard_map(local, mesh=mesh, in_specs=in_specs, out_specs=out_specs, check_vma=False)
```

```python
import math

import jax
import jax.numpy as jnp
from jax import lax
from jax.sharding import PartitionSpec as P


def from_behind(value, axis, steps):
    count = lax.axis_size(axis)
    pairs = [(source, (source + steps) % count) for source in range(count)]
    return lax.ppermute(value, axis, pairs)


def partner_pairs(axis, mask):
    return [(index, index ^ mask) for index in range(lax.axis_size(axis))]


def radix_digits(axis):
    bits = lax.axis_size(axis).bit_length() - 1
    widths = [1] * (bits % 2) + [2] * (bits // 2)
    lows = [sum(widths[:n]) for n in range(len(widths))]
    return [(axis, low, width) for low, width in zip(lows, widths)]


def digit_sum(value, digits):
    for axis, low, width in digits:
        count = 1 << width
        digit = (lax.axis_index(axis) >> low) & (count - 1)
        part = value.shape[0] // count
        total = lax.dynamic_slice_in_dim(value, digit * part, part, 0)
        for shift in range(1, count):
            send = lax.dynamic_slice_in_dim(value, (digit ^ shift) * part, part, 0)
            total = total + lax.ppermute(send, axis, partner_pairs(axis, shift << low))
        value = total
    return value


def digit_gather(value, digits):
    for axis, low, width in reversed(digits):
        count = 1 << width
        digit = (lax.axis_index(axis) >> low) & (count - 1)
        got = [value] + [
            lax.ppermute(value, axis, partner_pairs(axis, shift << low)) for shift in range(1, count)
        ]
        pieces = []
        for place in range(count):
            piece = got[0]
            for shift in range(1, count):
                piece = jnp.where((place ^ digit) == shift, got[shift], piece)
            pieces.append(piece)
        value = jnp.concatenate(pieces, 1)
    return value

def link_parts(raw_links):
    slice_count, wide_x, wide_y = (raw_links.shape[0], raw_links.shape[1], raw_links.shape[2])
    z_count = raw_links.shape[-1] // 2
    split = raw_links.reshape(slice_count, wide_x, wide_y, 3, 3, 3, 2, z_count)
    moved = jnp.transpose(split, (3, 6, 0, 1, 2, 7, 4, 5))
    return (moved[:, 0], moved[:, 1])


def color_apply(real_links, imag_links, vectors, dagger):
    pattern = "...ba,...bpk->...apk" if dagger else "...ab,...bpk->...apk"
    real_term = jnp.einsum(pattern, real_links, vectors, preferred_element_type=jnp.float32)
    imag_term = jnp.einsum(pattern, imag_links, vectors, preferred_element_type=jnp.float32)
    if dagger:
        imag_term = -imag_term
    real_out = real_term[..., 0, :] - imag_term[..., 1, :]
    imag_out = real_term[..., 1, :] + imag_term[..., 0, :]
    return jnp.stack([real_out, imag_out], axis=-2)


def phase_parts(momentum, coord_x, coord_y, coord_z, span_x, span_y, span_z):
    fraction = (jnp.mod(momentum[0] * coord_x, span_x).astype(jnp.float32) / span_x)[:, None, None]
    fraction = (
        fraction
        + (jnp.mod(momentum[1] * coord_y, span_y).astype(jnp.float32) / span_y)[None, :, None]
    )
    fraction = (
        fraction
        + (jnp.mod(momentum[2] * coord_z, span_z).astype(jnp.float32) / span_z)[None, None, :]
    )
    phase_angle = 2.0 * math.pi * fraction
    return (jnp.cos(phase_angle)[..., None, None], jnp.sin(phase_angle)[..., None, None])


def complex_product(left_side, right_side):
    half_width = left_side.shape[-2]
    highest = lax.Precision.HIGHEST
    left_real, left_imag = (left_side[..., :half_width], left_side[..., half_width:])
    right_real, right_imag = (right_side[..., :half_width], right_side[..., half_width:])
    real_out = jnp.matmul(left_real, right_real, precision=highest) - jnp.matmul(
        left_imag, right_imag, precision=highest
    )
    imag_out = jnp.matmul(left_real, right_imag, precision=highest) + jnp.matmul(
        left_imag, right_real, precision=highest
    )
    return jnp.concatenate([real_out, imag_out], axis=-1)


def local(eigvecs, links, momenta, directions, pairs, perambulators):
    slices, cells_x, cells_y, cells_z = (
        eigvecs.shape[0],
        eigvecs.shape[1],
        eigvecs.shape[2],
        eigvecs.shape[3],
    )
    mode_count = eigvecs.shape[-1] // 2
    op_count = momenta.shape[0]
    span_x = cells_x * lax.axis_size("gx")
    span_y = cells_y * lax.axis_size("gy")
    scale_norm = 1.0 / math.sqrt(3 * span_x * span_y * cells_z)
    planes = jnp.transpose(eigvecs[0], (0, 1, 3, 2, 4))
    vec_wide = planes.astype(jnp.float32)
    link_wide = jnp.transpose(
        links[0].reshape(cells_x, cells_y, 3, 3, 3, 2, cells_z), (2, 5, 0, 1, 3, 4, 6)
    ).astype(jnp.float32)
    row_count = cells_x * cells_y * cells_z * 3

    def colour_apply(direction, vectors, dagger):
        real_links, imag_links = (link_wide[direction, 0], link_wide[direction, 1])
        if dagger:
            real_links = jnp.swapaxes(real_links, 2, 3)
            imag_links = jnp.swapaxes(imag_links, 2, 3)
        real_term = sum(real_links[:, :, :, b, :, None] * vectors[:, :, None, b] for b in range(3))
        imag_term = sum(imag_links[:, :, :, b, :, None] * vectors[:, :, None, b] for b in range(3))
        if dagger:
            imag_term = -imag_term
        turned = jnp.concatenate([-imag_term[..., mode_count:], imag_term[..., :mode_count]], -1)
        return real_term + turned

    ahead_x = from_behind(planes[:1], "gx", -1).astype(jnp.float32)
    next_x = jnp.concatenate([vec_wide[1:], ahead_x], axis=0)
    back_x = colour_apply(0, vec_wide, True).astype(jnp.bfloat16)
    prev_x = jnp.concatenate([from_behind(back_x[-1:], "gx", 1), back_x[:-1]], axis=0)
    ahead_y = from_behind(planes[:, :1], "gy", -1).astype(jnp.float32)
    next_y = jnp.concatenate([vec_wide[:, 1:], ahead_y], axis=1)
    back_y = colour_apply(1, vec_wide, True).astype(jnp.bfloat16)
    prev_y = jnp.concatenate([from_behind(back_y[:, -1:], "gy", 1), back_y[:, :-1]], axis=1)
    back_z = colour_apply(2, vec_wide, True).astype(jnp.bfloat16)
    prev_z = jnp.roll(back_z, 1, axis=3)
    displaced = [
        (colour_apply(0, next_x, False) - prev_x.astype(jnp.float32)).astype(jnp.bfloat16),
        (colour_apply(1, next_y, False) - prev_y.astype(jnp.float32)).astype(jnp.bfloat16),
        (colour_apply(2, jnp.roll(vec_wide, -1, axis=3), False) - prev_z.astype(jnp.float32)).astype(
            jnp.bfloat16
        ),
    ]
    stacked = jnp.stack(displaced).reshape(3, row_count, 2 * mode_count)
    coord_x = lax.axis_index("gx") * cells_x + jnp.arange(cells_x, dtype=jnp.int32)
    coord_y = lax.axis_index("gy") * cells_y + jnp.arange(cells_y, dtype=jnp.int32)
    coord_z = jnp.arange(cells_z, dtype=jnp.int32)
    cosine, sine_part = jax.vmap(
        lambda momentum: phase_parts(momentum, coord_x, coord_y, coord_z, span_x, span_y, cells_z)
    )(momenta)
    row_shape = (op_count, cells_x, cells_y, 3, cells_z, 1)
    site_shape = (op_count, cells_x, cells_y, 1, cells_z, 1)
    row_cosine = jnp.broadcast_to(cosine.reshape(site_shape), row_shape).reshape(op_count, row_count, 1)
    row_sine = jnp.broadcast_to(sine_part.reshape(site_shape), row_shape).reshape(op_count, row_count, 1)
    vec_rows = planes.reshape(row_count, 2 * mode_count)
    vec_real = vec_rows[:, :mode_count]
    vec_imag = vec_rows[:, mode_count:]
    cosine_side = jnp.concatenate([vec_real, -vec_imag], axis=-1).astype(jnp.float32)
    sine_side = jnp.concatenate([-vec_imag, -vec_real], axis=-1).astype(jnp.float32)
    weighted = (row_cosine * cosine_side[None] + row_sine * sine_side[None]).astype(jnp.bfloat16)
    chosen = jnp.take(stacked, directions, axis=0, mode="clip")
    blocks = jnp.einsum("ork,orm->okm", weighted, chosen, preferred_element_type=jnp.float32)
    field_real = blocks[:, :mode_count, :mode_count] - blocks[:, mode_count:, mode_count:]
    field_imag = blocks[:, :mode_count, mode_count:] + blocks[:, mode_count:, :mode_count]
    partial_sum = jnp.concatenate([field_real, field_imag], axis=-1)[None]
    flat_sum = partial_sum.reshape(-1, partial_sum.shape[-1])
    digits = radix_digits("gy") + radix_digits("gx")
    reduced = digit_sum(flat_sum, digits) * scale_norm
    other_part = lax.ppermute(reduced, "ta", [(0, 1), (1, 0)])
    both_parts = jnp.where(
        lax.axis_index("ta") == 0,
        jnp.stack([reduced, other_part]),
        jnp.stack([other_part, reduced]),
    )
    whole_field = digit_gather(both_parts, digits).reshape(
        (2,) + partial_sum.shape[1:]
    )
    own_fields = lax.dynamic_index_in_dim(whole_field, lax.axis_index("ta"), 0, keepdims=True)
    highest = lax.Precision.HIGHEST
    sink_field = jnp.take(whole_field, pairs[:, 0], axis=0, mode="clip")
    source_field = jnp.take(whole_field, pairs[:, 1], axis=0, mode="clip")
    prop_real = perambulators[..., :mode_count]
    prop_imag = perambulators[..., mode_count:]
    prop_block = jnp.concatenate(
        [perambulators, jnp.concatenate([-prop_imag, prop_real], axis=-1)], axis=-2
    )
    left_product = jnp.einsum("poik,pkj->poij", sink_field, prop_block, precision=highest)
    source_block = jnp.concatenate(
        [
            source_field,
            jnp.concatenate(
                [-source_field[..., mode_count:], source_field[..., :mode_count]], axis=-1
            ),
        ],
        axis=-2,
    )
    right_product = jnp.einsum("pik,pokj->poij", perambulators, source_block, precision=highest)
    correlator = jnp.einsum("paij,pbij->pab", left_product, right_product, precision=highest)
    correlator = (correlator / (mode_count * mode_count)).reshape(
        pairs.shape[0], op_count * op_count
    )
    return (own_fields, correlator)


def solution(mesh):
    in_specs = (
        P("ta", "gx", "gy", None, None, None),
        P("ta", "gx", "gy", None, None, None, None),
        P(),
        P(),
        P(("gx", "gy", "ta"), None),
        P(("gx", "gy", "ta"), None, None),
    )
    out_specs = (P("ta", None, None, None), P(("gx", "gy", "ta"), None))
    return jax.shard_map(local, mesh=mesh, in_specs=in_specs, out_specs=out_specs, check_vma=False)
```
